512 devices in a mesh: row: 32 (over x, z), col: 16 (over y, core).
Axes of the slice: x: 4, y: 8, z: 8, core: 2. Of those that a mesh axis runs over, the one named last changes fastest.
Arguments:
- basis_now: float32 [131072, 128], P(('row', 'col')), may hold values from -6 to 6
- basis_prev: float32 [131072, 128], P(('row', 'col')), may hold values from -6 to 6
- coupling: float32 [128, 128], replicated, may hold values from -0.875 to 0.875
- tiles: bfloat16 [32, 16, 16, 128, 128], P('row', 'col'), may hold values from -0.1875 to 0.1875
- tile_rows: int32 [32, 16, 16], P('row', 'col'), may hold values from 0 to 63
- tile_cols: int32 [32, 16, 16], P('row', 'col'), may hold values from 0 to 31
- tile_counts: int32 [32, 16], P('row', 'col'), may hold values from 4 to 16, as said below
Outputs:
- basis: float32 [131072, 128], P(('row', 'col'))
- projection: float32 [128, 128], replicated
- rfactor: float32 [128, 128], replicated
The draws below stay inside these ranges and needn't reach their ends.
Inputs may be any that keep to these rules, and one draw needn't show every extreme that they name: Each device uses the first tile_counts of its 16 tile slots; some device uses all of them.
All inputs are finite; a program needn't handle non-finite values.
Results may differ from the reference program's by a relative error of at most 0.0033.
Values may be sent and summed in bfloat16 or wider, within the bound.
A program may use at most 64 MiB of HBM per device.

```python
import jax
import jax.numpy as jnp
from jax import lax

B = 128
TILE = 128
NV = 256
TMAX = 16
NROWS = 131072
RTILES = 64
CTILES = 32
N_ROW = 32
N_COL = 16


def draw_tile_counts(key, part):
    key_counts, key_full = jax.random.split(key)
    counts = jax.random.randint(key_counts, (N_ROW * N_COL,), TMAX // 4, TMAX + 1)
    fullest = jax.random.randint(key_full, (), 0, N_ROW * N_COL)
    flattened = jnp.where(jnp.arange(N_ROW * N_COL) == fullest, TMAX, counts)
    return flattened.reshape(N_ROW, N_COL).astype(jnp.int32)


def place_ends(result, rng, low, top_value):
    dims = result.shape
    place = [jax.random.randint(jax.random.fold_in(rng, axis), (), 0, dims[axis]) for axis in range(len(dims))]
    result = result.at[tuple(place)].set(low)
    longest = dims.index(max(dims))
    place[longest] = (place[longest] + 1) % dims[longest]
    return result.at[tuple(place)].set(top_value)


def steps_of(rng, dims, pieces, least, top_value):
    def one(position, shards_of):
        draws = jax.random.uniform(jax.random.fold_in(jax.random.fold_in(rng, 6), position), (shards_of,), jnp.float32, least / len(pieces), top_value / len(pieces))
        return jnp.repeat(jnp.exp(draws), dims[position] // shards_of).reshape((-1,) + (1,) * (len(dims) - position - 1))

    level = one(*pieces[0])
    for cut in pieces[1:]:
        level = level * one(*cut)
    return level


def bell_draw(key, shape, spread, limit, cuts=(), kind=jnp.bfloat16):
    result = jax.random.normal(key, shape, jnp.float32) * spread
    if len(cuts) > 0:
        result = steps_of(key, shape, cuts, -0.22, 0.18) * result
    return jnp.clip(result, min=-limit, max=limit).astype(kind)


def setup_inputs(seed: int = 0) -> dict:
    key_of = jax.random.split(jax.random.key(seed), 8)
    basis_now = bell_draw(key_of[0], (NROWS, B), 1.0, 6.0, ((0, 512),), jnp.float32)
    basis_prev = bell_draw(key_of[1], (NROWS, B), 1.0, 6.0, ((0, 512),), jnp.float32)
    coupling = bell_draw(key_of[2], (B, B), (0.7 * B ** -0.5), 0.875, (), jnp.float32)
    tiles = bell_draw(key_of[3], (N_ROW, N_COL, TMAX, TILE, TILE), (TMAX * TILE * TILE // NV) ** -0.5, 0.1875, ((0, 32), (1, 16)))
    tile_rows = place_ends(jax.random.randint(key_of[4], (N_ROW, N_COL, TMAX), 0, RTILES), jax.random.fold_in(key_of[4], 1), 0, RTILES - 1).astype(jnp.int32)
    tile_cols = place_ends(jax.random.randint(key_of[5], (N_ROW, N_COL, TMAX), 0, CTILES), jax.random.fold_in(key_of[5], 1), 0, CTILES - 1).astype(jnp.int32)
    tile_counts = draw_tile_counts(jax.random.fold_in(key_of[7], 71), 0)
    return dict(basis_now=basis_now, basis_prev=basis_prev, coupling=coupling, tiles=tiles, tile_rows=tile_rows, tile_cols=tile_cols, tile_counts=tile_counts)


HIGHEST = lax.Precision.HIGHEST

def upper_cholesky(gram):
    return jnp.linalg.cholesky(gram).T

def lower_inverse(lower_part):
    identity = jnp.eye(lower_part.shape[0], dtype=lower_part.dtype)
    return jax.scipy.linalg.solve_triangular(lower_part, identity, lower=True)

def tile_product(tile_block, row_ids, col_ids, tile_total, column_basis):
    stacked = column_basis.reshape(-1, TILE, B)
    chosen = stacked[col_ids]
    products = jnp.einsum('tij,tjb->tib', tile_block.astype(jnp.float32), chosen.astype(jnp.float32))
    usable = jnp.arange(TMAX, dtype=jnp.int32) < tile_total
    selector = (row_ids[None, :] == jnp.arange(RTILES, dtype=jnp.int32)[:, None]) & usable[None, :]
    partial_value = jnp.einsum('rt,tib->rib', selector.astype(jnp.float32), products, precision=HIGHEST)
    return partial_value.reshape(RTILES * TILE, B)

def reference(basis_now, basis_prev, coupling, tiles, tile_rows, tile_cols, tile_counts):
    half_basis = basis_now.astype(jnp.bfloat16)
    column_blocks = half_basis.reshape(N_ROW, N_COL * NV, B)

    def column(col_index):

        def accumulate(running, row_index):
            partial_value = tile_product(tiles[row_index, col_index], tile_rows[row_index, col_index], tile_cols[row_index, col_index], tile_counts[row_index, col_index], column_blocks[row_index])
            return (running + partial_value, None)
        running, _ = lax.scan(accumulate, jnp.zeros((N_ROW * NV, B), jnp.float32), jnp.arange(N_ROW, dtype=jnp.int32))
        return running
    blocks = lax.map(column, jnp.arange(N_COL, dtype=jnp.int32))
    product = blocks.reshape(N_COL, N_ROW, NV, B).transpose(1, 0, 2, 3).reshape(NROWS, B)
    norm_scale = float(NROWS) ** (-0.5)
    projection = jnp.dot(basis_now.T, product, precision=HIGHEST) * norm_scale
    upper_part = jnp.triu(coupling)
    residual = product - jnp.dot(basis_now, projection, precision=HIGHEST) * norm_scale
    residual = residual - jnp.dot(basis_prev, upper_part.T, precision=HIGHEST)
    gram = jnp.dot(residual.T, residual, precision=HIGHEST) / float(NROWS)
    rfactor = upper_cholesky(gram)
    inverse = lower_inverse(rfactor.T)
    basis = jnp.dot(residual, inverse.T, precision=HIGHEST)
    return (basis, projection, rfactor)
```

```python
import functools

import jax
import jax.numpy as jnp
from jax import lax
from jax.experimental import pallas as pl
from jax.experimental.pallas import tpu as pltpu
from jax.sharding import PartitionSpec as P

HIGHEST = lax.Precision.HIGHEST
MESH = pl.DeviceIdType.MESH
F32 = jnp.float32
BF16 = jnp.bfloat16

NX, NZ, NY, NC = 4, 8, 8, 2
SLOTS = 16
T = 128
AHEAD = (4, 3, 2, 1)
BEHIND = (0, -3, -2, -1)


def dot(a, b, dims):
    return lax.dot_general(a, b, (dims, ((), ())), precision=HIGHEST, preferred_element_type=F32)


def step_kernel(
    rows_ref, cols_ref, count_ref, v_ref, vp_ref, coupling_ref, tiles_ref,
    residual_ref, projection_ref, gram_ref,
    latest, half, gathered, sums, sums16, prev_part, vt,
    fwd, direct, comb, fwd_in, direct_in, comb_in,
    own, zsend, zsend4, zrecv, zrecv4, part,
    red1, red2, red3, piece1, piece2, piece3, totals,
    ring_s, ring_r, pair_s, pair_r, x_s, x_r, z_s, z_r,
    r1_s, r1_r, r2_s, r2_r, r3_s, r3_r, r4_s, r4_r,
):
    row = lax.axis_index("row")
    col = lax.axis_index("col")
    x, z = row // NZ, row % NZ
    y, core = col // NC, col % NC

    def at(dx=0, dz=0, dy=0, dc=0):
        return (
            ((x + dx + NX) % NX) * NZ + (z + dz + NZ) % NZ,
            ((y + dy + NY) % NY) * NC + (core + dc) % NC,
        )

    def copy(src, dst, send, recv, device):
        return pltpu.make_async_remote_copy(
            src_ref=src, dst_ref=dst, send_sem=send, recv_sem=recv, device_id=device, device_id_type=MESH
        )

    barrier = pltpu.get_barrier_semaphore()
    peers = [at(dz=d // 2, dc=d % 2) for d in range(1, 16)]
    peers += [at(dy=d) for d in range(1, NY)] + [at(dx=d) for d in range(1, NX)]
    for peer in peers:
        pl.semaphore_signal(barrier, inc=1, device_id=peer, device_id_type=MESH)

    half[...] = v_ref[...].astype(BF16).reshape(2, T, T)
    pl.semaphore_wait(barrier, len(peers))

    pending = []

    def start(c):
        c.start()
        pending.append(c)
        return c

    def block(origin, h, c):
        return gathered.at[2 * (NC * origin + c) + h]

    def ring(direction, step, h):
        origin = (y - direction * (step - 1) + NY) % NY
        dst = block(origin, h, core)
        src = half.at[h] if step == 1 else dst
        d = 0 if direction == 1 else 1
        return copy(src, dst, ring_s.at[d, step - 1, h], ring_r.at[d, step - 1, h], at(dy=direction))

    def arrived(direction, step, h):
        origin = (y - direction * step + NY) % NY
        d = 0 if direction == 1 else 1
        dst = block(origin, h, core)
        return copy(dst, dst, ring_s.at[d, step - 1, h], ring_r.at[d, step - 1, h], at(dy=direction))

    def to_pair(delta, h):
        origin = (y + delta + NY) % NY
        dst = block(origin, h, core)
        src = half.at[h] if delta == 0 else dst
        k = (delta + NY) % NY
        return copy(src, dst, pair_s.at[k, h], pair_r.at[k, h], at(dc=1))

    def from_pair(delta, h):
        origin = (y + delta + NY) % NY
        dst = block(origin, h, 1 - core)
        k = (delta + NY) % NY
        return copy(dst, dst, pair_s.at[k, h], pair_r.at[k, h], at(dc=1))

    def has(direction, step, h):
        return step < 4 or (step == 4 and (h == 0) == (direction == 1))

    for h in range(2):
        for direction in (1, -1):
            start(ring(direction, 1, h))
    for h in range(2):
        start(to_pair(0, h))

    gathered[pl.ds(2 * col, 2)] = half[...]
    i0 = lax.broadcasted_iota(jnp.int32, (T, T), 0)
    i1 = lax.broadcasted_iota(jnp.int32, (T, T), 1)
    upper = jnp.where(i0 <= i1, coupling_ref[...], 0.0)
    prev_part[...] = dot(vp_ref[...], upper, ((1,), (1,)))
    vt[...] = v_ref[...].T
    sums[SLOTS] = jnp.zeros((T, T), F32)
    sums16[SLOTS] = jnp.zeros((T, T), BF16)
    count = count_ref[0]
    used = [jnp.where(t < count, rows_ref[t], -1) for t in range(SLOTS)]

    def find(r, carry):
        found = jnp.int32(SLOTS)
        for t in range(SLOTS):
            found = jnp.where(used[t] == r, t, found)
        latest[r] = found
        return carry

    lax.fori_loop(0, NX * NZ * 2, find, 0)

    for step in range(1, 5):
        for h in range(2):
            for direction in (1, -1):
                if has(direction, step, h):
                    arrived(direction, step, h).wait_recv()
                    if has(direction, step + 1, h):
                        start(ring(direction, step + 1, h))
                    start(to_pair(-direction * step, h))
    for delta in range(NY):
        for h in range(2):
            from_pair(delta, h).wait_recv()

    for t in range(SLOTS):
        before = jnp.int32(SLOTS)
        for s in range(t):
            before = jnp.where(used[s] == used[t], s, before)
        value = sums[before] + jnp.dot(tiles_ref[t], gathered[cols_ref[t]], preferred_element_type=F32)
        sums[t] = value
        sums16[t] = value.astype(BF16)

    def tile_of(dx, dz, h):
        return 2 * (((x + dx + NX) % NX) * NZ + (z + dz + NZ) % NZ) + h

    def fill(dst, dx, dz):
        for h in range(2):
            dst[h] = sums16[latest[tile_of(dx, dz, h)]]

    def xcopy(kind, s, k):
        src = (fwd, direct, comb)[kind].at[s, k]
        dst = (fwd_in, direct_in, comb_in)[kind].at[s, k]
        return copy(src, dst, x_s.at[kind, s, k], x_r.at[kind, s, k], at(dx=1 if s == 0 else -1))

    side = (AHEAD, BEHIND)

    def send_forward(k):
        for s in range(2):
            fill(fwd.at[s, k], 2, side[s][k])
            start(xcopy(0, s, k))

    def send_direct(k):
        for s in range(2):
            fill(direct.at[s, k], 1 if s == 0 else -1, side[1 - s][k])
            start(xcopy(1, s, k))

    def send_combined(k):
        for s in range(2):
            xcopy(0, s, k).wait_recv()
            for h in range(2):
                mine = sums[latest[tile_of(1 if s == 0 else -1, side[s][k], h)]]
                comb[s, k, h] = (mine + fwd_in[s, k, h].astype(F32)).astype(BF16)
            start(xcopy(2, s, k))

    def zcopy(s, k):
        if k == 0:
            return copy(zsend4.at[s], zrecv4.at[s], z_s.at[s, 0], z_r.at[s, 0], at(dz=1 if s == 0 else -1))
        return copy(zsend.at[s, k - 1], zrecv.at[s, k - 1], z_s.at[s, k], z_r.at[s, k], at(dz=1 if s == 0 else -1))

    def line_sum(s, k, h):
        mine = sums[latest[tile_of(0, side[s][k], h)]]
        return mine + comb_in[s, k, h].astype(F32) + direct_in[1 - s, k, h].astype(F32)

    def finish(k):
        for s in range(2):
            xcopy(2, s, k).wait_recv()
            xcopy(1, 1 - s, k).wait_recv()
            if k == 0:
                if s == 0:
                    for h in range(2):
                        zsend4[h] = line_sum(0, 0, h)
                        start(zcopy(h, 0))
                else:
                    for h in range(2):
                        own[h] = line_sum(1, 0, h)
            else:
                zcopy(s, k - 1).wait_recv()
                for h in range(2):
                    value = line_sum(s, k, h)
                    if k > 1:
                        value = value + zrecv[s, k - 2, h]
                    elif h == s:
                        value = value + zrecv4[s]
                    zsend[s, k - 1, h] = value
                start(zcopy(s, k))

    send_forward(0)
    send_direct(0)
    send_forward(1)
    send_direct(1)
    send_combined(0)
    send_forward(2)
    send_direct(2)
    finish(0)
    send_combined(1)
    send_forward(3)
    send_direct(3)
    finish(1)
    send_combined(2)
    finish(2)
    send_combined(3)
    finish(3)
    for s in range(2):
        zcopy(s, 3).wait_recv()
    product = (own[...] + zrecv[0, 2] + zrecv[1, 2]).reshape(2 * T, T)

    g = z * NC + core

    def group_peer(d):
        h = (g + d) % SLOTS
        return h, (x * NZ + h // NC, y * NC + h % NC)

    def total(n, out_ref):
        for d in range(1, SLOTS):
            h, device = group_peer(d)
            start(copy(part.at[n, pl.ds(8 * h, 8)], red1.at[n, g], r1_s.at[n, d], r1_r.at[n, d], device))
        red1[n, g] = part[n, pl.ds(8 * g, 8)]
        for d in range(1, SLOTS):
            h, device = group_peer(SLOTS - d)
            copy(red1.at[n, h], red1.at[n, h], r1_s.at[n, d], r1_r.at[n, d], device).wait_recv()
        piece1[n] = jnp.sum(red1[n], axis=0)
        for d in range(1, NY):
            start(copy(piece1.at[n], red2.at[n, y], r2_s.at[n, d], r2_r.at[n, d], at(dy=d)))
        red2[n, y] = piece1[n]
        for d in range(1, NY):
            other = (y + NY - d) % NY
            copy(red2.at[n, other], red2.at[n, other], r2_s.at[n, d], r2_r.at[n, d], at(dy=NY - d)).wait_recv()
        piece2[n] = jnp.sum(red2[n], axis=0)
        for d in range(1, NX):
            start(copy(piece2.at[n], red3.at[n, x], r3_s.at[n, d], r3_r.at[n, d], at(dx=d)))
        red3[n, x] = piece2[n]
        for d in range(1, NX):
            other = (x + NX - d) % NX
            copy(red3.at[n, other], red3.at[n, other], r3_s.at[n, d], r3_r.at[n, d], at(dx=NX - d)).wait_recv()
        piece3[n] = jnp.sum(red3[n], axis=0)
        mine = totals.at[n, pl.ds(8 * g, 8)]
        for d in range(1, SLOTS):
            h, device = group_peer(d)
            start(copy(piece3.at[n], mine, r4_s.at[n, d], r4_r.at[n, d], device))
        totals[n, pl.ds(8 * g, 8)] = piece3[n]
        for d in range(1, SLOTS):
            h, device = group_peer(SLOTS - d)
            theirs = totals.at[n, pl.ds(8 * h, 8)]
            copy(theirs, theirs, r4_s.at[n, d], r4_r.at[n, d], device).wait_recv()
        return totals[n]

    scale = float(NX * NZ * NY * NC * 2 * T) ** (-0.5)
    part[0] = dot(vt[...], product, ((1,), (0,)))
    projection = total(0, projection_ref) * scale
    projection_ref[...] = projection
    residual = product - dot(v_ref[...], projection, ((1,), (0,))) * scale - prev_part[...]
    residual_ref[...] = residual
    part[1] = dot(residual, residual, ((0,), (0,)))
    gram_ref[...] = total(1, gram_ref) * (scale * scale)

    for c in pending:
        c.wait_send()


def communicate(rows, cols, count, v, vp, coupling, tiles):
    vmem = pl.BlockSpec(memory_space=pltpu.VMEM)
    smem = pl.BlockSpec(memory_space=pltpu.SMEM)
    dma = pltpu.SemaphoreType.DMA
    pair = (2, 4, 2, T, T)
    return pl.pallas_call(
        step_kernel,
        out_shape=(
            jax.ShapeDtypeStruct((2 * T, T), F32),
            jax.ShapeDtypeStruct((T, T), F32),
            jax.ShapeDtypeStruct((T, T), F32),
        ),
        in_specs=[smem, smem, smem, vmem, vmem, vmem, vmem],
        out_specs=(vmem, vmem, vmem),
        scratch_shapes=[
            pltpu.SMEM((NX * NZ * 2,), jnp.int32),
            pltpu.VMEM((2, T, T), BF16),
            pltpu.VMEM((2 * SLOTS, T, T), BF16),
            pltpu.VMEM((SLOTS + 1, T, T), F32),
            pltpu.VMEM((SLOTS + 1, T, T), BF16),
            pltpu.VMEM((2 * T, T), F32),
            pltpu.VMEM((T, 2 * T), F32),
        ]
        + [pltpu.VMEM(pair, BF16)] * 6
        + [
            pltpu.VMEM((2, T, T), F32),
            pltpu.VMEM((2, 3, 2, T, T), F32),
            pltpu.VMEM((2, T, T), F32),
            pltpu.VMEM((2, 3, 2, T, T), F32),
            pltpu.VMEM((2, T, T), F32),
            pltpu.VMEM((2, T, T), F32),
            pltpu.VMEM((2, SLOTS, 8, T), F32),
            pltpu.VMEM((2, NY, 8, T), F32),
            pltpu.VMEM((2, NX, 8, T), F32),
            pltpu.VMEM((2, 8, T), F32),
            pltpu.VMEM((2, 8, T), F32),
            pltpu.VMEM((2, 8, T), F32),
            pltpu.VMEM((2, T, T), F32),
            dma((2, 4, 2)), dma((2, 4, 2)), dma((NY, 2)), dma((NY, 2)),
            dma((3, 2, 4)), dma((3, 2, 4)), dma((2, 4)), dma((2, 4)),
            dma((2, SLOTS)), dma((2, SLOTS)), dma((2, NY)), dma((2, NY)),
            dma((2, NX)), dma((2, NX)), dma((2, SLOTS)), dma((2, SLOTS)),
        ],
        compiler_params=pltpu.CompilerParams(collective_id=0, has_side_effects=True),
        name="krylov_step",
    )(rows, cols, count, v, vp, coupling, tiles)


def on_device(basis_now, basis_prev, coupling, tiles, tile_rows, tile_cols, tile_counts):
    residual, projection, gram = communicate(
        tile_rows[0, 0], tile_cols[0, 0], tile_counts[0], basis_now, basis_prev, coupling, tiles[0, 0]
    )
    rfactor = jnp.linalg.cholesky(gram).T
    identity = jnp.eye(T, dtype=F32)
    inverse = jax.scipy.linalg.solve_triangular(rfactor.T, identity, lower=True)
    basis = jnp.dot(residual, inverse.T, precision=HIGHEST)
    return (basis, projection, rfactor)


def solution(mesh):
    placed = (
        P(("row", "col"), None),
        P(("row", "col"), None),
        P(),
        P("row", "col", None, None, None),
        P("row", "col", None),
        P("row", "col", None),
        P("row", "col"),
    )
    return jax.shard_map(
        on_device,
        mesh=mesh,
        in_specs=placed,
        out_specs=(P(("row", "col"), None), P(), P()),
        check_vma=False,
    )
```

```python
import functools

import jax
import jax.numpy as jnp
from jax import lax
from jax.experimental import pallas as pl
from jax.experimental.pallas import tpu as pltpu
from jax.sharding import PartitionSpec as P

HIGHEST = lax.Precision.HIGHEST
MESH = pl.DeviceIdType.MESH
F32 = jnp.float32
BF16 = jnp.bfloat16

NX, NZ, NY, NC = 4, 8, 8, 2
SLOTS = 16
T = 128
AHEAD = (4, 3, 2, 1)
BEHIND = (0, -3, -2, -1)


def dot(a, b, dims):
    return lax.dot_general(a, b, (dims, ((), ())), precision=HIGHEST, preferred_element_type=F32)


def step_kernel(
    rows_ref, cols_ref, count_ref, v_ref, vp_ref, coupling_ref, tiles_ref,
    open_ref, late_ref, early_ref,
    v_s, vp_s, coupling_s, tiles_s, local_sem,
    latest, before, half, gathered, sums, sums16, prev_part, vt,
    fwd, direct, comb, fwd_in, direct_in, comb_in,
    own, zsend, zsend4, zrecv, zrecv4, part,
    red1, red2, red3, piece1, piece2, piece3, totals,
    ring_s, ring_r, pair_s, pair_r, x_s, x_r, z_s, z_r,
    r1_s, r1_r, r2_s, r2_r, r3_s, r3_r, r4_s, r4_r,
):
    row = lax.axis_index("row")
    col = lax.axis_index("col")
    x, z = row // NZ, row % NZ
    y, core = col // NC, col % NC

    def at(dx=0, dz=0, dy=0, dc=0):
        return (
            ((x + dx + NX) % NX) * NZ + (z + dz + NZ) % NZ,
            ((y + dy + NY) % NY) * NC + (core + dc) % NC,
        )

    def copy(src, dst, send, recv, device):
        return pltpu.make_async_remote_copy(
            src_ref=src, dst_ref=dst, send_sem=send, recv_sem=recv, device_id=device, device_id_type=MESH
        )

    barrier = pltpu.get_barrier_semaphore()
    peers = [at(dz=d // 2, dc=d % 2) for d in range(1, 16)]
    peers += [at(dy=d) for d in range(1, NY)] + [at(dx=d) for d in range(1, NX)]
    for peer in peers:
        pl.semaphore_signal(barrier, inc=1, device_id=peer, device_id_type=MESH)

    loads = [
        pltpu.make_async_copy(src, dst, local_sem.at[i])
        for i, (src, dst) in enumerate(
            ((v_ref, v_s), (vp_ref, vp_s), (coupling_ref, coupling_s), (tiles_ref, tiles_s))
        )
    ]
    for load in loads:
        load.start()
    loads[0].wait()
    half[...] = v_s[...].astype(BF16).reshape(2, T, T)
    pl.semaphore_wait(barrier, len(peers))

    pending = []

    def start(c):
        c.start()
        pending.append(c)
        return c

    def block(origin, h, c):
        return gathered.at[2 * (NC * origin + c) + h]

    def ring(direction, step, h):
        origin = (y - direction * (step - 1) + NY) % NY
        dst = block(origin, h, core)
        src = half.at[h] if step == 1 else dst
        d = 0 if direction == 1 else 1
        return copy(src, dst, ring_s.at[d, step - 1, h], ring_r.at[d, step - 1, h], at(dy=direction))

    def arrived(direction, step, h):
        origin = (y - direction * step + NY) % NY
        d = 0 if direction == 1 else 1
        dst = block(origin, h, core)
        return copy(dst, dst, ring_s.at[d, step - 1, h], ring_r.at[d, step - 1, h], at(dy=direction))

    def to_pair(delta, h):
        origin = (y + delta + NY) % NY
        dst = block(origin, h, core)
        src = half.at[h] if delta == 0 else dst
        k = (delta + NY) % NY
        return copy(src, dst, pair_s.at[k, h], pair_r.at[k, h], at(dc=1))

    def from_pair(delta, h):
        origin = (y + delta + NY) % NY
        dst = block(origin, h, 1 - core)
        k = (delta + NY) % NY
        return copy(dst, dst, pair_s.at[k, h], pair_r.at[k, h], at(dc=1))

    def has(direction, step, h):
        return step < 4 or (step == 4 and (h == 0) == (direction == 1))

    for h in range(2):
        for direction in (1, -1):
            start(ring(direction, 1, h))
    for h in range(2):
        start(to_pair(0, h))

    g = z * NC + core

    def group_peer(d):
        h = (g + d) % SLOTS
        return h, (x * NZ + h // NC, y * NC + h % NC)

    def scatter(n):
        for d in range(1, SLOTS):
            h, device = group_peer(d)
            start(copy(part.at[n, pl.ds(16 * h, 16)], red1.at[n, g], r1_s.at[n, d], r1_r.at[n, d], device))
        red1[n, g] = part[n, pl.ds(16 * g, 16)]

    def over_y(n):
        for d in range(1, SLOTS):
            h, device = group_peer(SLOTS - d)
            copy(red1.at[n, h], red1.at[n, h], r1_s.at[n, d], r1_r.at[n, d], device).wait_recv()
        piece1[n] = jnp.sum(red1[n], axis=0)
        for d in range(1, NY):
            start(copy(piece1.at[n], red2.at[n, y], r2_s.at[n, d], r2_r.at[n, d], at(dy=d)))
        red2[n, y] = piece1[n]

    def over_x(n):
        for d in range(1, NY):
            other = (y + NY - d) % NY
            copy(red2.at[n, other], red2.at[n, other], r2_s.at[n, d], r2_r.at[n, d], at(dy=NY - d)).wait_recv()
        piece2[n] = jnp.sum(red2[n], axis=0)
        for d in range(1, NX):
            start(copy(piece2.at[n], red3.at[n, x], r3_s.at[n, d], r3_r.at[n, d], at(dx=d)))
        red3[n, x] = piece2[n]

    def back(n):
        for d in range(1, NX):
            other = (x + NX - d) % NX
            copy(red3.at[n, other], red3.at[n, other], r3_s.at[n, d], r3_r.at[n, d], at(dx=NX - d)).wait_recv()
        piece3[n] = jnp.sum(red3[n], axis=0)
        mine = totals.at[n, pl.ds(16 * g, 16)]
        for d in range(1, SLOTS):
            h, device = group_peer(d)
            start(copy(piece3.at[n], mine, r4_s.at[n, d], r4_r.at[n, d], device))
        totals[n, pl.ds(16 * g, 16)] = piece3[n]

    def collect(n):
        for d in range(1, SLOTS):
            h, device = group_peer(SLOTS - d)
            theirs = totals.at[n, pl.ds(16 * h, 16)]
            copy(theirs, theirs, r4_s.at[n, d], r4_r.at[n, d], device).wait_recv()

    def pass_on(step):
        for h in range(2):
            for direction in (1, -1):
                if has(direction, step, h):
                    arrived(direction, step, h).wait_recv()
                    if has(direction, step + 1, h):
                        start(ring(direction, step + 1, h))
                    start(to_pair(-direction * step, h))

    gathered[pl.ds(2 * col, 2)] = half[...]
    loads[1].wait()
    loads[2].wait()
    i0 = lax.broadcasted_iota(jnp.int32, (T, T), 0)
    i1 = lax.broadcasted_iota(jnp.int32, (T, T), 1)
    upper = jnp.where(i0 <= i1, coupling_s[...], 0.0)
    prev_part[...] = dot(vp_s[...], upper, ((1,), (1,)))
    vt[...] = v_s[...].T
    pass_on(1)

    part[1, 0:T] = dot(vt[...], v_s[...], ((1,), (0,)))
    part[1, T : 2 * T] = dot(vt[...], prev_part[...], ((1,), (0,)))
    scatter(1)
    pass_on(2)

    sums[SLOTS] = jnp.zeros((T, T), F32)
    sums16[SLOTS] = jnp.zeros((T, T), BF16)
    count = count_ref[0]
    used = [jnp.where(t < count, rows_ref[t], -1) for t in range(SLOTS)]

    def find(r, carry):
        found = jnp.int32(SLOTS)
        for t in range(SLOTS):
            found = jnp.where(used[t] == r, t, found)
        latest[r] = found
        return carry

    lax.fori_loop(0, NX * NZ, find, 0)
    pass_on(3)

    lax.fori_loop(NX * NZ, NX * NZ * 2, find, 0)
    for t in range(SLOTS):
        found = jnp.int32(SLOTS)
        for s in range(t):
            found = jnp.where(used[s] == used[t], s, found)
        before[t] = found
    loads[3].wait()
    pass_on(4)
    for delta in range(NY):
        for h in range(2):
            from_pair(delta, h).wait_recv()

    for t in range(SLOTS):
        value = sums[before[t]] + jnp.dot(tiles_s[t], gathered[cols_ref[t]], preferred_element_type=F32)
        sums[t] = value
        sums16[t] = value.astype(BF16)

    def tile_of(dx, dz, h):
        return 2 * (((x + dx + NX) % NX) * NZ + (z + dz + NZ) % NZ) + h

    def fill(dst, dx, dz):
        for h in range(2):
            dst[h] = sums16[latest[tile_of(dx, dz, h)]]

    def xcopy(kind, s, k):
        src = (fwd, direct, comb)[kind].at[s, k]
        dst = (fwd_in, direct_in, comb_in)[kind].at[s, k]
        return copy(src, dst, x_s.at[kind, s, k], x_r.at[kind, s, k], at(dx=1 if s == 0 else -1))

    side = (AHEAD, BEHIND)

    def send_forward(k):
        for s in range(2):
            fill(fwd.at[s, k], 2, side[s][k])
            start(xcopy(0, s, k))

    def send_direct(k):
        for s in range(2):
            fill(direct.at[s, k], 1 if s == 0 else -1, side[1 - s][k])
            start(xcopy(1, s, k))

    def send_combined(k):
        for s in range(2):
            xcopy(0, s, k).wait_recv()
            for h in range(2):
                mine = sums[latest[tile_of(1 if s == 0 else -1, side[s][k], h)]]
                comb[s, k, h] = (mine + fwd_in[s, k, h].astype(F32)).astype(BF16)
            start(xcopy(2, s, k))

    def zcopy(s, k):
        if k == 0:
            return copy(zsend4.at[s], zrecv4.at[s], z_s.at[s, 0], z_r.at[s, 0], at(dz=1 if s == 0 else -1))
        return copy(zsend.at[s, k - 1], zrecv.at[s, k - 1], z_s.at[s, k], z_r.at[s, k], at(dz=1 if s == 0 else -1))

    def line_sum(s, k, h):
        mine = sums[latest[tile_of(0, side[s][k], h)]]
        return mine + comb_in[s, k, h].astype(F32) + direct_in[1 - s, k, h].astype(F32)

    def finish(k):
        for s in range(2):
            xcopy(2, s, k).wait_recv()
            xcopy(1, 1 - s, k).wait_recv()
            if k == 0:
                if s == 0:
                    for h in range(2):
                        zsend4[h] = line_sum(0, 0, h)
                        start(zcopy(h, 0))
                else:
                    for h in range(2):
                        own[h] = line_sum(1, 0, h)
            else:
                zcopy(s, k - 1).wait_recv()
                for h in range(2):
                    value = line_sum(s, k, h)
                    if k > 1:
                        value = value + zrecv[s, k - 2, h]
                    elif h == s:
                        value = value + zrecv4[s]
                    zsend[s, k - 1, h] = value
                start(zcopy(s, k))

    send_forward(0)
    send_direct(0)
    send_forward(1)
    send_direct(1)
    over_y(1)
    send_combined(0)
    send_forward(2)
    send_direct(2)
    finish(0)
    over_x(1)
    send_combined(1)
    send_forward(3)
    send_direct(3)
    finish(1)
    back(1)
    send_combined(2)
    finish(2)
    send_combined(3)
    finish(3)
    for s in range(2):
        zcopy(s, 3).wait_recv()
    product = (own[...] + zrecv[0, 2] + zrecv[1, 2]).reshape(2 * T, T)

    opened = product - prev_part[...]
    part[0, 0:T] = dot(vt[...], product, ((1,), (0,)))
    part[0, T : 2 * T] = dot(opened, opened, ((0,), (0,)))
    scatter(0)
    open_ref[...] = opened
    collect(1)
    early_ref[...] = totals[1]
    over_y(0)
    over_x(0)
    back(0)
    collect(0)
    late_ref[...] = totals[0]

    for c in pending:
        c.wait_send()


def communicate(rows, cols, count, v, vp, coupling, tiles):
    vmem = pl.BlockSpec(memory_space=pltpu.VMEM)
    smem = pl.BlockSpec(memory_space=pltpu.SMEM)
    dma = pltpu.SemaphoreType.DMA
    pair = (2, 4, 2, T, T)
    return pl.pallas_call(
        step_kernel,
        out_shape=(
            jax.ShapeDtypeStruct((2 * T, T), F32),
            jax.ShapeDtypeStruct((2 * T, T), F32),
            jax.ShapeDtypeStruct((2 * T, T), F32),
        ),
        in_specs=[smem, smem, smem] + [pl.BlockSpec(memory_space=pl.ANY)] * 4,
        out_specs=(vmem, vmem, vmem),
        scratch_shapes=[
            pltpu.VMEM((2 * T, T), F32),
            pltpu.VMEM((2 * T, T), F32),
            pltpu.VMEM((T, T), F32),
            pltpu.VMEM((SLOTS, T, T), BF16),
            dma((4,)),
            pltpu.SMEM((NX * NZ * 2,), jnp.int32),
            pltpu.SMEM((SLOTS,), jnp.int32),
            pltpu.VMEM((2, T, T), BF16),
            pltpu.VMEM((2 * SLOTS, T, T), BF16),
            pltpu.VMEM((SLOTS + 1, T, T), F32),
            pltpu.VMEM((SLOTS + 1, T, T), BF16),
            pltpu.VMEM((2 * T, T), F32),
            pltpu.VMEM((T, 2 * T), F32),
        ]
        + [pltpu.VMEM(pair, BF16)] * 6
        + [
            pltpu.VMEM((2, T, T), F32),
            pltpu.VMEM((2, 3, 2, T, T), F32),
            pltpu.VMEM((2, T, T), F32),
            pltpu.VMEM((2, 3, 2, T, T), F32),
            pltpu.VMEM((2, T, T), F32),
            pltpu.VMEM((2, 2 * T, T), F32),
            pltpu.VMEM((2, SLOTS, 16, T), F32),
            pltpu.VMEM((2, NY, 16, T), F32),
            pltpu.VMEM((2, NX, 16, T), F32),
            pltpu.VMEM((2, 16, T), F32),
            pltpu.VMEM((2, 16, T), F32),
            pltpu.VMEM((2, 16, T), F32),
            pltpu.VMEM((2, 2 * T, T), F32),
            dma((2, 4, 2)), dma((2, 4, 2)), dma((NY, 2)), dma((NY, 2)),
            dma((3, 2, 4)), dma((3, 2, 4)), dma((2, 4)), dma((2, 4)),
            dma((2, SLOTS)), dma((2, SLOTS)), dma((2, NY)), dma((2, NY)),
            dma((2, NX)), dma((2, NX)), dma((2, SLOTS)), dma((2, SLOTS)),
        ],
        compiler_params=pltpu.CompilerParams(collective_id=0, has_side_effects=True),
        name="krylov_step",
    )(rows, cols, count, v, vp, coupling, tiles)


def factor_kernel(total, late_ref, early_ref, open_ref, v_ref, basis_ref, projection_ref, rfactor_ref, residual, inverse_ref):
    image = late_ref[0:T]
    along = image * (1.0 / total)
    projection_ref[...] = image * total ** (-0.5)
    residual[...] = open_ref[...] - dot(v_ref[...], along, ((1,), (0,)))
    inner = (image - early_ref[T : 2 * T]) * (1.0 / total)
    inner = inner - 0.5 * dot(early_ref[0:T] * (1.0 / total), along, ((1,), (0,)))
    cross = dot(along, inner, ((0,), (0,)))
    gram = late_ref[T : 2 * T] * (1.0 / total) - cross - cross.T
    lane = lax.broadcasted_iota(jnp.int32, (1, T), 1)
    groups = T // 8
    left = [gram[8 * i : 8 * i + 8] for i in range(groups)]
    sub8 = lax.broadcasted_iota(jnp.int32, (8, T), 0)
    lane8 = lax.broadcasted_iota(jnp.int32, (8, T), 1)
    right = [jnp.where(lane8 == sub8 + 8 * i, 1.0, 0.0).astype(F32) for i in range(groups)]

    def spread(row):
        return jnp.broadcast_to(row, (8, T))

    for p in range(groups):
        panel, other = left[p], right[p]
        columns = [jnp.broadcast_to(panel[:, 8 * p + j : 8 * p + j + 1], (8, T)) for j in range(8)]
        a = [[spread(columns[j][i : i + 1]) for j in range(i + 1)] for i in range(8)]
        inv = [[None] * 8 for _ in range(8)]
        low = [[None] * 8 for _ in range(8)]
        for j in range(8):
            inv[j][j] = lax.rsqrt(a[j][j])
            for i in range(j + 1, 8):
                low[i][j] = a[i][j] * inv[j][j]
            for i in range(j + 1, 8):
                for k in range(j + 1, i + 1):
                    a[i][k] = a[i][k] - low[i][j] * low[k][j]
            for k in range(j):
                s = low[j][k] * inv[k][k]
                for m in range(k + 1, j):
                    s = s + low[j][m] * inv[m][k]
                inv[j][k] = -(s * inv[j][j])
        rows_l = [spread(panel[j : j + 1]) for j in range(8)]
        rows_r = [spread(other[j : j + 1]) for j in range(8)]

        def mix(rows, weight, picks):
            value = None
            for j in picks:
                term = weight(j) * rows[j]
                value = term if value is None else value + term
            return value

        out_l = [mix(rows_l, lambda j, i=i: inv[i][j], range(i + 1)) for i in range(8)]
        out_r = [mix(rows_r, lambda j, i=i: inv[i][j], range(i + 1)) for i in range(8)]
        for i in range(8):
            r = 8 * p + i
            rfactor_ref[pl.ds(r, 1)] = jnp.where(lane >= r, out_l[i][0:1], 0.0)
            inverse_ref[pl.ds(r, 1)] = out_r[i][0:1]
        if p + 1 < groups:
            back_l = [mix(out_l, lambda i, j=j: inv[i][j], range(j, 8)) for j in range(8)]
            back_r = [mix(out_r, lambda i, j=j: inv[i][j], range(j, 8)) for j in range(8)]
            for g in range(p + 1, groups):
                cols = [jnp.broadcast_to(left[g][:, 8 * p + j : 8 * p + j + 1], (8, T)) for j in range(8)]
                left[g] = left[g] - mix(back_l, lambda j: cols[j], range(8))
                right[g] = right[g] - mix(back_r, lambda j: cols[j], range(8))
    basis_ref[...] = dot(residual[...], inverse_ref[...], ((1,), (1,)))


def factor(total, late, early, opened, v):
    vmem = pl.BlockSpec(memory_space=pltpu.VMEM)
    return pl.pallas_call(
        functools.partial(factor_kernel, total),
        out_shape=(
            jax.ShapeDtypeStruct((2 * T, T), F32),
            jax.ShapeDtypeStruct((T, T), F32),
            jax.ShapeDtypeStruct((T, T), F32),
        ),
        in_specs=[vmem] * 4,
        out_specs=(vmem,) * 3,
        scratch_shapes=[pltpu.VMEM((2 * T, T), F32), pltpu.VMEM((T, T), F32)],
        name="factor",
    )(late, early, opened, v)


def on_device(basis_now, basis_prev, coupling, tiles, tile_rows, tile_cols, tile_counts):
    opened, late, early = communicate(
        tile_rows[0, 0], tile_cols[0, 0], tile_counts[0], basis_now, basis_prev, coupling, tiles[0, 0]
    )
    total = float(NX * NZ * NY * NC * 2 * T)
    return factor(total, late, early, opened, basis_now)


def solution(mesh):
    placed = (
        P(("row", "col"), None),
        P(("row", "col"), None),
        P(),
        P("row", "col", None, None, None),
        P("row", "col", None),
        P("row", "col", None),
        P("row", "col"),
    )
    return jax.shard_map(
        on_device,
        mesh=mesh,
        in_specs=placed,
        out_specs=(P(("row", "col"), None), P(), P()),
        check_vma=False,
    )
```

```python
import functools

import jax
import jax.numpy as jnp
from jax import lax
from jax.experimental import pallas as pl
from jax.experimental.pallas import tpu as pltpu
from jax.sharding import PartitionSpec as P

HIGHEST = lax.Precision.HIGHEST
MESH = pl.DeviceIdType.MESH
F32 = jnp.float32
BF16 = jnp.bfloat16

NX, NZ, NY, NC = 4, 8, 8, 2
SLOTS = 16
T = 128
AHEAD = (4, 3, 2, 1)
BEHIND = (-3, -2, -1, 0)


def dot(a, b, dims):
    return lax.dot_general(a, b, (dims, ((), ())), precision=HIGHEST, preferred_element_type=F32)


def step_kernel(
    rows_ref, cols_ref, count_ref, v_ref, vp_ref, coupling_ref, tiles_ref,
    open_ref, late_ref, early_ref,
    v_s, vp_s, coupling_s, tiles_s, local_sem,
    latest, before, half, gathered, sums, sums16, prev_part, vt,
    fwd, direct, comb, fwd_in, direct_in, comb_in,
    own, zsend, zrecv, part,
    red1, red2, red3, piece1, piece2, piece3, totals,
    ring_s, ring_r, pair_s, pair_r, x_s, x_r, z_s, z_r,
    r1_s, r1_r, r2_s, r2_r, r3_s, r3_r, r4_s, r4_r,
):
    row = lax.axis_index("row")
    col = lax.axis_index("col")
    x, z = row // NZ, row % NZ
    y, core = col // NC, col % NC

    def at(dx=0, dz=0, dy=0, dc=0):
        return (
            ((x + dx + NX) % NX) * NZ + (z + dz + NZ) % NZ,
            ((y + dy + NY) % NY) * NC + (core + dc) % NC,
        )

    def copy(src, dst, send, recv, device):
        return pltpu.make_async_remote_copy(
            src_ref=src, dst_ref=dst, send_sem=send, recv_sem=recv, device_id=device, device_id_type=MESH
        )

    barrier = pltpu.get_barrier_semaphore()
    peers = [at(dz=d // 2, dc=d % 2) for d in range(1, 16)]
    peers += [at(dy=d) for d in range(1, NY)] + [at(dx=d) for d in range(1, NX)]
    for peer in peers:
        pl.semaphore_signal(barrier, inc=1, device_id=peer, device_id_type=MESH)

    loads = [
        pltpu.make_async_copy(src, dst, local_sem.at[i])
        for i, (src, dst) in enumerate(
            ((v_ref, v_s), (vp_ref, vp_s), (coupling_ref, coupling_s), (tiles_ref, tiles_s))
        )
    ]
    for load in loads:
        load.start()
    loads[0].wait()
    half[...] = v_s[...].astype(BF16).reshape(2, T, T)
    pl.semaphore_wait(barrier, len(peers))

    pending = []

    def start(c):
        c.start()
        pending.append(c)
        return c

    def block(origin, h, c):
        return gathered.at[2 * (NC * origin + c) + h]

    def along(direction, far, h):
        d = 0 if direction == 1 else 1
        if far <= 2:
            src, dst, device = half.at[h], block(y, h, core), at(dy=far * direction)
        else:
            dst = block((y - 2 * direction + NY) % NY, h, core)
            src, device = dst, at(dy=(far - 2) * direction)
        return copy(src, dst, ring_s.at[d, far - 1, h], ring_r.at[d, far - 1, h], device)

    def arrived(direction, far, h):
        d = 0 if direction == 1 else 1
        dst = block((y - direction * far + NY) % NY, h, core)
        return copy(dst, dst, ring_s.at[d, far - 1, h], ring_r.at[d, far - 1, h], at(dy=direction))

    def to_pair(delta, h):
        origin = (y + delta + NY) % NY
        dst = block(origin, h, core)
        src = half.at[h] if delta == 0 else dst
        k = (delta + NY) % NY
        return copy(src, dst, pair_s.at[k, h], pair_r.at[k, h], at(dc=1))

    def from_pair(delta, h):
        origin = (y + delta + NY) % NY
        dst = block(origin, h, 1 - core)
        k = (delta + NY) % NY
        return copy(dst, dst, pair_s.at[k, h], pair_r.at[k, h], at(dc=1))

    def has(direction, far, h):
        return far < 4 or (h == 0) == (direction == 1)

    for far in (2, 1):
        for h in range(2):
            for direction in (1, -1):
                start(along(direction, far, h))
    for h in range(2):
        start(to_pair(0, h))

    g = z * NC + core

    def group_peer(d):
        h = (g + d) % SLOTS
        return h, (x * NZ + h // NC, y * NC + h % NC)

    def scatter(n):
        for d in range(1, SLOTS):
            h, device = group_peer(d)
            start(copy(part.at[n, pl.ds(16 * h, 16)], red1.at[n, g], r1_s.at[n, d], r1_r.at[n, d], device))
        red1[n, g] = part[n, pl.ds(16 * g, 16)]

    def over_y(n):
        for d in range(1, SLOTS):
            h, device = group_peer(SLOTS - d)
            copy(red1.at[n, h], red1.at[n, h], r1_s.at[n, d], r1_r.at[n, d], device).wait_recv()
        piece1[n] = jnp.sum(red1[n], axis=0)
        for d in range(1, NY):
            start(copy(piece1.at[n], red2.at[n, y], r2_s.at[n, d], r2_r.at[n, d], at(dy=d)))
        red2[n, y] = piece1[n]

    def over_x(n):
        for d in range(1, NY):
            other = (y + NY - d) % NY
            copy(red2.at[n, other], red2.at[n, other], r2_s.at[n, d], r2_r.at[n, d], at(dy=NY - d)).wait_recv()
        piece2[n] = jnp.sum(red2[n], axis=0)
        for d in range(1, NX):
            start(copy(piece2.at[n], red3.at[n, x], r3_s.at[n, d], r3_r.at[n, d], at(dx=d)))
        red3[n, x] = piece2[n]

    def back(n):
        for d in range(1, NX):
            other = (x + NX - d) % NX
            copy(red3.at[n, other], red3.at[n, other], r3_s.at[n, d], r3_r.at[n, d], at(dx=NX - d)).wait_recv()
        piece3[n] = jnp.sum(red3[n], axis=0)
        mine = totals.at[n, pl.ds(16 * g, 16)]
        for d in range(1, SLOTS):
            h, device = group_peer(d)
            start(copy(piece3.at[n], mine, r4_s.at[n, d], r4_r.at[n, d], device))
        totals[n, pl.ds(16 * g, 16)] = piece3[n]

    def collect(n):
        for d in range(1, SLOTS):
            h, device = group_peer(SLOTS - d)
            theirs = totals.at[n, pl.ds(16 * h, 16)]
            copy(theirs, theirs, r4_s.at[n, d], r4_r.at[n, d], device).wait_recv()

    def take(far):
        for h in range(2):
            for direction in (1, -1):
                if has(direction, far, h):
                    arrived(direction, far, h).wait_recv()
                    if far == 2:
                        start(along(direction, 3, h))
                        if has(direction, 4, h):
                            start(along(direction, 4, h))
                    start(to_pair(-direction * far, h))

    gathered[pl.ds(2 * col, 2)] = half[...]
    loads[1].wait()
    loads[2].wait()
    i0 = lax.broadcasted_iota(jnp.int32, (T, T), 0)
    i1 = lax.broadcasted_iota(jnp.int32, (T, T), 1)
    upper = jnp.where(i0 <= i1, coupling_s[...], 0.0)
    prev_part[...] = dot(vp_s[...], upper, ((1,), (1,)))
    vt[...] = v_s[...].T
    take(2)

    part[1, 0:T] = dot(vt[...], v_s[...], ((1,), (0,)))
    part[1, T : 2 * T] = dot(vt[...], prev_part[...], ((1,), (0,)))
    scatter(1)
    take(1)

    sums[SLOTS] = jnp.zeros((T, T), F32)
    sums16[SLOTS] = jnp.zeros((T, T), BF16)
    count = count_ref[0]
    used = [jnp.where(t < count, rows_ref[t], -1) for t in range(SLOTS)]

    def find(r, carry):
        found = jnp.int32(SLOTS)
        for t in range(SLOTS):
            found = jnp.where(used[t] == r, t, found)
        latest[r] = found
        return carry

    lax.fori_loop(0, NX * NZ * 2, find, 0)
    for t in range(SLOTS):
        found = jnp.int32(SLOTS)
        for s in range(t):
            found = jnp.where(used[s] == used[t], s, found)
        before[t] = found
    loads[3].wait()
    take(3)
    take(4)
    for delta in range(NY):
        for h in range(2):
            from_pair(delta, h).wait_recv()

    for t in range(SLOTS):
        value = sums[before[t]] + jnp.dot(tiles_s[t], gathered[cols_ref[t]], preferred_element_type=F32)
        sums[t] = value
        sums16[t] = value.astype(BF16)

    def tile_of(dx, dz, h):
        return 2 * (((x + dx + NX) % NX) * NZ + (z + dz + NZ) % NZ) + h

    def fill(dst, dx, dz):
        for h in range(2):
            dst[h] = sums16[latest[tile_of(dx, dz, h)]]

    def xcopy(kind, s, k):
        src = (fwd, direct, comb)[kind].at[s, k]
        dst = (fwd_in, direct_in, comb_in)[kind].at[s, k]
        return copy(src, dst, x_s.at[kind, s, k], x_r.at[kind, s, k], at(dx=1 if s == 0 else -1))

    side = (AHEAD, BEHIND)

    def send_forward(k):
        for s in range(2):
            fill(fwd.at[s, k], 2, side[s][k])
            start(xcopy(0, s, k))

    def send_direct(k):
        for s in range(2):
            fill(direct.at[s, k], 1 if s == 0 else -1, side[1 - s][k])
            start(xcopy(1, s, k))

    def send_combined(k):
        for s in range(2):
            xcopy(0, s, k).wait_recv()
            for h in range(2):
                mine = sums[latest[tile_of(1 if s == 0 else -1, side[s][k], h)]]
                comb[s, k, h] = (mine + fwd_in[s, k, h].astype(F32)).astype(BF16)
            start(xcopy(2, s, k))

    def zcopy(s, k):
        return copy(zsend.at[s, k], zrecv.at[s, k], z_s.at[s, k], z_r.at[s, k], at(dz=side[s][k]))

    def line_sum(s, k, h):
        mine = sums[latest[tile_of(0, side[s][k], h)]]
        return mine + comb_in[s, k, h].astype(F32) + direct_in[1 - s, k, h].astype(F32)

    def finish(k):
        for s in range(2):
            xcopy(2, s, k).wait_recv()
            xcopy(1, 1 - s, k).wait_recv()
            for h in range(2):
                if side[s][k] == 0:
                    own[h] = line_sum(s, k, h)
                else:
                    zsend[s, k, h] = line_sum(s, k, h).astype(BF16)
            if side[s][k] != 0:
                start(zcopy(s, k))

    send_forward(0)
    send_direct(0)
    send_forward(1)
    send_direct(1)
    over_y(1)
    send_combined(0)
    send_forward(2)
    send_direct(2)
    send_combined(1)
    send_forward(3)
    send_direct(3)
    finish(0)
    over_x(1)
    send_combined(2)
    finish(1)
    send_combined(3)
    back(1)
    finish(2)
    finish(3)
    product = own[...]
    for k in range(4):
        for s in range(2):
            if side[s][k] != 0:
                zcopy(s, k).wait_recv()
                product = product + zrecv[s, k].astype(F32)
    product = product.reshape(2 * T, T)

    opened = product - prev_part[...]
    part[0, 0:T] = dot(vt[...], product, ((1,), (0,)))
    part[0, T : 2 * T] = dot(opened, opened, ((0,), (0,)))
    scatter(0)
    open_ref[...] = opened
    collect(1)
    early_ref[...] = totals[1]
    over_y(0)
    over_x(0)
    back(0)
    collect(0)
    late_ref[...] = totals[0]

    for c in pending:
        c.wait_send()


def communicate(rows, cols, count, v, vp, coupling, tiles):
    vmem = pl.BlockSpec(memory_space=pltpu.VMEM)
    smem = pl.BlockSpec(memory_space=pltpu.SMEM)
    dma = pltpu.SemaphoreType.DMA
    pair = (2, 4, 2, T, T)
    return pl.pallas_call(
        step_kernel,
        out_shape=(
            jax.ShapeDtypeStruct((2 * T, T), F32),
            jax.ShapeDtypeStruct((2 * T, T), F32),
            jax.ShapeDtypeStruct((2 * T, T), F32),
        ),
        in_specs=[smem, smem, smem] + [pl.BlockSpec(memory_space=pl.ANY)] * 4,
        out_specs=(vmem, vmem, vmem),
        scratch_shapes=[
            pltpu.VMEM((2 * T, T), F32),
            pltpu.VMEM((2 * T, T), F32),
            pltpu.VMEM((T, T), F32),
            pltpu.VMEM((SLOTS, T, T), BF16),
            dma((4,)),
            pltpu.SMEM((NX * NZ * 2,), jnp.int32),
            pltpu.SMEM((SLOTS,), jnp.int32),
            pltpu.VMEM((2, T, T), BF16),
            pltpu.VMEM((2 * SLOTS, T, T), BF16),
            pltpu.VMEM((SLOTS + 1, T, T), F32),
            pltpu.VMEM((SLOTS + 1, T, T), BF16),
            pltpu.VMEM((2 * T, T), F32),
            pltpu.VMEM((T, 2 * T), F32),
        ]
        + [pltpu.VMEM(pair, BF16)] * 6
        + [
            pltpu.VMEM((2, T, T), F32),
            pltpu.VMEM(pair, BF16),
            pltpu.VMEM(pair, BF16),
            pltpu.VMEM((2, 2 * T, T), F32),
            pltpu.VMEM((2, SLOTS, 16, T), F32),
            pltpu.VMEM((2, NY, 16, T), F32),
            pltpu.VMEM((2, NX, 16, T), F32),
            pltpu.VMEM((2, 16, T), F32),
            pltpu.VMEM((2, 16, T), F32),
            pltpu.VMEM((2, 16, T), F32),
            pltpu.VMEM((2, 2 * T, T), F32),
            dma((2, 4, 2)), dma((2, 4, 2)), dma((NY, 2)), dma((NY, 2)),
            dma((3, 2, 4)), dma((3, 2, 4)), dma((2, 4)), dma((2, 4)),
            dma((2, SLOTS)), dma((2, SLOTS)), dma((2, NY)), dma((2, NY)),
            dma((2, NX)), dma((2, NX)), dma((2, SLOTS)), dma((2, SLOTS)),
        ],
        compiler_params=pltpu.CompilerParams(collective_id=0, has_side_effects=True),
        name="krylov_step",
    )(rows, cols, count, v, vp, coupling, tiles)


def factor_kernel(total, late_ref, early_ref, open_ref, v_ref, basis_ref, projection_ref, rfactor_ref, residual, inverse_ref):
    image = late_ref[0:T]
    along = image * (1.0 / total)
    projection_ref[...] = image * total ** (-0.5)
    residual[...] = open_ref[...] - dot(v_ref[...], along, ((1,), (0,)))
    inner = (image - early_ref[T : 2 * T]) * (1.0 / total)
    inner = inner - 0.5 * dot(early_ref[0:T] * (1.0 / total), along, ((1,), (0,)))
    cross = dot(along, inner, ((0,), (0,)))
    gram = late_ref[T : 2 * T] * (1.0 / total) - cross - cross.T
    lane = lax.broadcasted_iota(jnp.int32, (1, T), 1)
    groups = T // 8
    left = [gram[8 * i : 8 * i + 8] for i in range(groups)]
    sub8 = lax.broadcasted_iota(jnp.int32, (8, T), 0)
    lane8 = lax.broadcasted_iota(jnp.int32, (8, T), 1)
    right = [jnp.where(lane8 == sub8 + 8 * i, 1.0, 0.0).astype(F32) for i in range(groups)]

    def spread(row):
        return jnp.broadcast_to(row, (8, T))

    for p in range(groups):
        panel, other = left[p], right[p]
        columns = [jnp.broadcast_to(panel[:, 8 * p + j : 8 * p + j + 1], (8, T)) for j in range(8)]
        a = [[spread(columns[j][i : i + 1]) for j in range(i + 1)] for i in range(8)]
        inv = [[None] * 8 for _ in range(8)]
        low = [[None] * 8 for _ in range(8)]
        for j in range(8):
            inv[j][j] = lax.rsqrt(a[j][j])
            for i in range(j + 1, 8):
                low[i][j] = a[i][j] * inv[j][j]
            for i in range(j + 1, 8):
                for k in range(j + 1, i + 1):
                    a[i][k] = a[i][k] - low[i][j] * low[k][j]
            for k in range(j):
                s = low[j][k] * inv[k][k]
                for m in range(k + 1, j):
                    s = s + low[j][m] * inv[m][k]
                inv[j][k] = -(s * inv[j][j])
        rows_l = [spread(panel[j : j + 1]) for j in range(8)]
        rows_r = [spread(other[j : j + 1]) for j in range(8)]

        def mix(rows, weight, picks):
            value = None
            for j in picks:
                term = weight(j) * rows[j]
                value = term if value is None else value + term
            return value

        out_l = [mix(rows_l, lambda j, i=i: inv[i][j], range(i + 1)) for i in range(8)]
        out_r = [mix(rows_r, lambda j, i=i: inv[i][j], range(i + 1)) for i in range(8)]
        for i in range(8):
            r = 8 * p + i
            rfactor_ref[pl.ds(r, 1)] = jnp.where(lane >= r, out_l[i][0:1], 0.0)
            inverse_ref[pl.ds(r, 1)] = out_r[i][0:1]
        if p + 1 < groups:
            back_l = [mix(out_l, lambda i, j=j: inv[i][j], range(j, 8)) for j in range(8)]
            back_r = [mix(out_r, lambda i, j=j: inv[i][j], range(j, 8)) for j in range(8)]
            for g in range(p + 1, groups):
                cols = [jnp.broadcast_to(left[g][:, 8 * p + j : 8 * p + j + 1], (8, T)) for j in range(8)]
                left[g] = left[g] - mix(back_l, lambda j: cols[j], range(8))
                right[g] = right[g] - mix(back_r, lambda j: cols[j], range(8))
    basis_ref[...] = dot(residual[...], inverse_ref[...], ((1,), (1,)))


def factor(total, late, early, opened, v):
    vmem = pl.BlockSpec(memory_space=pltpu.VMEM)
    return pl.pallas_call(
        functools.partial(factor_kernel, total),
        out_shape=(
            jax.ShapeDtypeStruct((2 * T, T), F32),
            jax.ShapeDtypeStruct((T, T), F32),
            jax.ShapeDtypeStruct((T, T), F32),
        ),
        in_specs=[vmem] * 4,
        out_specs=(vmem,) * 3,
        scratch_shapes=[pltpu.VMEM((2 * T, T), F32), pltpu.VMEM((T, T), F32)],
        name="factor",
    )(late, early, opened, v)


def on_device(basis_now, basis_prev, coupling, tiles, tile_rows, tile_cols, tile_counts):
    opened, late, early = communicate(
        tile_rows[0, 0], tile_cols[0, 0], tile_counts[0], basis_now, basis_prev, coupling, tiles[0, 0]
    )
    total = float(NX * NZ * NY * NC * 2 * T)
    return factor(total, late, early, opened, basis_now)


def solution(mesh):
    placed = (
        P(("row", "col"), None),
        P(("row", "col"), None),
        P(),
        P("row", "col", None, None, None),
        P("row", "col", None),
        P("row", "col", None),
        P("row", "col"),
    )
    return jax.shard_map(
        on_device,
        mesh=mesh,
        in_specs=placed,
        out_specs=(P(("row", "col"), None), P(), P()),
        check_vma=False,
    )
```

```python
import functools

import jax
import jax.numpy as jnp
from jax import lax
from jax.experimental import pallas as pl
from jax.experimental.pallas import tpu as pltpu
from jax.sharding import PartitionSpec as P

HIGHEST = lax.Precision.HIGHEST
MESH = pl.DeviceIdType.MESH
F32 = jnp.float32
BF16 = jnp.bfloat16

NX, NZ, NY, NC = 4, 8, 8, 2
SLOTS = 16
T = 128
AHEAD = (4, 3, 2, 1)
BEHIND = (0, -3, -2, -1)


def dot(a, b, dims):
    return lax.dot_general(a, b, (dims, ((), ())), precision=HIGHEST, preferred_element_type=F32)


def step_kernel(
    rows_ref, cols_ref, count_ref, v_ref, vp_ref, coupling_ref, tiles_ref,
    open_ref, late_ref, early_ref,
    v_s, vp_s, coupling_s, tiles_s, local_sem,
    latest, before, half, gathered, sums, sums16, prev_part, vt,
    fwd, direct, comb, fwd_in, direct_in, comb_in,
    own, zsend, zrecv, zhalf, zhalf_in,
    ring_s, ring_r, pair_s, pair_r, x_s, x_r, z_s, z_r, zh_s, zh_r,
    *sum_refs,
):
    row = lax.axis_index("row")
    col = lax.axis_index("col")
    x, z = row // NZ, row % NZ
    y, core = col // NC, col % NC

    def at(dx=0, dz=0, dy=0, dc=0):
        return (
            ((x + dx + NX) % NX) * NZ + (z + dz + NZ) % NZ,
            ((y + dy + NY) % NY) * NC + (core + dc) % NC,
        )

    def copy(src, dst, send, recv, device):
        return pltpu.make_async_remote_copy(
            src_ref=src, dst_ref=dst, send_sem=send, recv_sem=recv, device_id=device, device_id_type=MESH
        )

    barrier = pltpu.get_barrier_semaphore()
    peers = [at(dz=d // 2, dc=d % 2) for d in range(1, 16)]
    peers += [at(dy=d) for d in range(1, NY)] + [at(dx=d, dc=c) for d in range(1, NX) for c in range(2)]
    for peer in peers:
        pl.semaphore_signal(barrier, inc=1, device_id=peer, device_id_type=MESH)

    loads = [
        pltpu.make_async_copy(src, dst, local_sem.at[i])
        for i, (src, dst) in enumerate(
            ((v_ref, v_s), (vp_ref, vp_s), (coupling_ref, coupling_s), (tiles_ref, tiles_s))
        )
    ]
    for load in loads:
        load.start()
    loads[0].wait()
    half[...] = v_s[...].astype(BF16).reshape(2, T, T)
    pl.semaphore_wait(barrier, len(peers))

    pending = []

    def start(c):
        c.start()
        pending.append(c)
        return c

    def block(origin, h, c):
        return gathered.at[2 * (NC * origin + c) + h]

    def along(direction, far, h):
        d = 0 if direction == 1 else 1
        if far <= 2:
            src, dst, device = half.at[h], block(y, h, core), at(dy=far * direction)
        else:
            dst = block((y - 2 * direction + NY) % NY, h, core)
            src, device = dst, at(dy=(far - 2) * direction)
        return copy(src, dst, ring_s.at[d, far - 1, h], ring_r.at[d, far - 1, h], device)

    def arrived(direction, far, h):
        d = 0 if direction == 1 else 1
        dst = block((y - direction * far + NY) % NY, h, core)
        return copy(dst, dst, ring_s.at[d, far - 1, h], ring_r.at[d, far - 1, h], at(dy=direction))

    def to_pair(delta, h):
        origin = (y + delta + NY) % NY
        dst = block(origin, h, core)
        src = half.at[h] if delta == 0 else dst
        k = (delta + NY) % NY
        return copy(src, dst, pair_s.at[k, h], pair_r.at[k, h], at(dc=1))

    def from_pair(delta, h):
        origin = (y + delta + NY) % NY
        dst = block(origin, h, 1 - core)
        k = (delta + NY) % NY
        return copy(dst, dst, pair_s.at[k, h], pair_r.at[k, h], at(dc=1))

    def has(direction, far, h):
        return far < 4 or (h == 0) == (direction == 1)

    for far in (2, 1):
        for h in range(2):
            for direction in (1, -1):
                start(along(direction, far, h))
    for h in range(2):
        start(to_pair(0, h))

    class Sum:
        def __init__(self, refs, over_z):
            self.part, self.totals, self.red, self.piece, self.send, self.recv = (
                refs[0], refs[1], refs[2:5], refs[5:8], refs[8:12], refs[12:16]
            )
            self.over_z = over_z
            self.place = (z if over_z else x) * NC + core
            self.last = x if over_z else z
            self.group, self.size, _ = self.red[0].shape

        def member(self, d):
            h = (self.place + d) % self.group
            if self.over_z:
                return h, (x * NZ + h // NC, y * NC + h % NC)
            return h, ((h // NC) * NZ + z, y * NC + h % NC)

        def rows(self, ref, h):
            return ref.at[pl.ds(self.size * h, self.size)]

        def move(self, stage, d, src, dst, device):
            return copy(src, dst, self.send[stage].at[d], self.recv[stage].at[d], device)

        def scatter(self):
            for d in range(1, self.group):
                h, device = self.member(d)
                start(self.move(0, d, self.rows(self.part, h), self.red[0].at[self.place], device))
            self.red[0][self.place] = self.part[pl.ds(self.size * self.place, self.size)]

        def reduce(self, stage, i):
            red, piece = self.red[stage], self.piece[stage]
            n = red.shape[0]
            for d in range(1, n):
                slot = red.at[(i + n - d) % n]
                self.move(stage, d, slot, slot, at(dc=1)).wait_recv()
            piece[...] = jnp.sum(red[...], axis=0)
            return piece

        def spread(self, stage, piece, i, device_at):
            red = self.red[stage]
            for d in range(1, red.shape[0]):
                start(self.move(stage, d, piece, red.at[i], device_at(d)))
            red[i] = piece[...]

        def over_y(self):
            self.spread(1, self.reduce(0, self.place), y, lambda d: at(dy=d))

        def over_last(self):
            piece = self.reduce(1, y)
            self.spread(2, piece, self.last, (lambda d: at(dx=d)) if self.over_z else (lambda d: at(dz=d)))

        def back(self):
            piece = self.reduce(2, self.last)
            for d in range(1, self.group):
                h, device = self.member(d)
                start(self.move(3, d, piece, self.rows(self.totals, self.place), device))
            self.totals[pl.ds(self.size * self.place, self.size)] = piece[...]

        def collect(self):
            for d in range(1, self.group):
                slot = self.rows(self.totals, (self.place + self.group - d) % self.group)
                self.move(3, d, slot, slot, at(dc=1)).wait_recv()

    image, square, early = (Sum(sum_refs[16 * i : 16 * i + 16], over_z) for i, over_z in enumerate((True, False, True)))

    def take(far):
        for h in range(2):
            for direction in (1, -1):
                if has(direction, far, h):
                    arrived(direction, far, h).wait_recv()
                    if far == 2:
                        start(along(direction, 3, h))
                        if has(direction, 4, h):
                            start(along(direction, 4, h))
                    start(to_pair(-direction * far, h))

    gathered[pl.ds(2 * col, 2)] = half[...]
    loads[1].wait()
    loads[2].wait()
    i0 = lax.broadcasted_iota(jnp.int32, (T, T), 0)
    i1 = lax.broadcasted_iota(jnp.int32, (T, T), 1)
    upper = jnp.where(i0 <= i1, coupling_s[...], 0.0)
    prev_part[...] = dot(vp_s[...], upper, ((1,), (1,)))
    vt[...] = v_s[...].T
    early.part[0:T] = dot(vt[...], v_s[...], ((1,), (0,)))
    early.part[T : 2 * T] = dot(vt[...], prev_part[...], ((1,), (0,)))
    early.scatter()
    take(2)
    take(1)

    sums[SLOTS] = jnp.zeros((T, T), F32)
    sums16[SLOTS] = jnp.zeros((T, T), BF16)
    count = count_ref[0]
    used = [jnp.where(t < count, rows_ref[t], -1) for t in range(SLOTS)]

    def find(r, carry):
        found = jnp.int32(SLOTS)
        for t in range(SLOTS):
            found = jnp.where(used[t] == r, t, found)
        latest[r] = found
        return carry

    lax.fori_loop(0, NX * NZ * 2, find, 0)
    for t in range(SLOTS):
        found = jnp.int32(SLOTS)
        for s in range(t):
            found = jnp.where(used[s] == used[t], s, found)
        before[t] = found
    loads[3].wait()
    early.over_y()
    take(3)
    take(4)
    for delta in range(NY):
        for h in range(2):
            from_pair(delta, h).wait_recv()

    for t in range(SLOTS):
        value = sums[before[t]] + jnp.dot(tiles_s[t], gathered[cols_ref[t]], preferred_element_type=F32)
        sums[t] = value
        sums16[t] = value.astype(BF16)

    def tile_of(dx, dz, h):
        return 2 * (((x + dx + NX) % NX) * NZ + (z + dz + NZ) % NZ) + h

    def fill(dst, dx, dz):
        for h in range(2):
            dst[h] = sums16[latest[tile_of(dx, dz, h)]]

    def xcopy(kind, s, k):
        src = (fwd, direct, comb)[kind].at[s, k]
        dst = (fwd_in, direct_in, comb_in)[kind].at[s, k]
        return copy(src, dst, x_s.at[kind, s, k], x_r.at[kind, s, k], at(dx=1 if s == 0 else -1))

    side = (AHEAD, BEHIND)

    def send_forward(k):
        for s in range(2):
            fill(fwd.at[s, k], 2, side[s][k])
            start(xcopy(0, s, k))

    def send_direct(k):
        for s in range(2):
            fill(direct.at[s, k], 1 if s == 0 else -1, side[1 - s][k])
            start(xcopy(1, s, k))

    def send_combined(k):
        for s in range(2):
            xcopy(0, s, k).wait_recv()
            for h in range(2):
                mine = sums[latest[tile_of(1 if s == 0 else -1, side[s][k], h)]]
                comb[s, k, h] = (mine + fwd_in[s, k, h].astype(F32)).astype(BF16)
            start(xcopy(2, s, k))

    def zcopy(s, k):
        return copy(zsend.at[s, k], zrecv.at[s, k], z_s.at[s, k], z_r.at[s, k], at(dz=side[s][k]))

    def zhalf_copy(s):
        return copy(zhalf.at[s], zhalf_in.at[s], zh_s.at[s], zh_r.at[s], at(dz=1 if s == 0 else -1))

    def line_sum(s, k, h):
        mine = sums[latest[tile_of(0, side[s][k], h)]]
        return mine + comb_in[s, k, h].astype(F32) + direct_in[1 - s, k, h].astype(F32)

    def finish(k):
        for s in range(2):
            xcopy(2, s, k).wait_recv()
            xcopy(1, 1 - s, k).wait_recv()
            if k == 1:
                zhalf_copy(s).wait_recv()
            for h in range(2):
                value = line_sum(s, k, h)
                if k == 0 and s == 0:
                    zhalf[h] = value.astype(BF16)
                    start(zhalf_copy(h))
                elif k == 0:
                    own[h] = value
                else:
                    if k == 1 and h == s:
                        value = value + zhalf_in[s].astype(F32)
                    zsend[s, k, h] = value.astype(BF16)
            if k > 0:
                start(zcopy(s, k))

    send_forward(0)
    send_forward(1)
    send_direct(0)
    send_forward(2)
    early.over_last()
    send_combined(0)
    send_direct(1)
    send_forward(3)
    send_combined(1)
    early.back()
    send_direct(2)
    finish(0)
    send_combined(2)
    send_direct(3)
    finish(1)
    send_combined(3)
    finish(2)
    finish(3)
    product = own[...]
    for k in range(1, 4):
        for s in range(2):
            zcopy(s, k).wait_recv()
            product = product + zrecv[s, k].astype(F32)
    product = product.reshape(2 * T, T)

    opened = product - prev_part[...]
    image.part[...] = dot(vt[...], product, ((1,), (0,)))
    image.scatter()
    square.part[...] = dot(opened, opened, ((0,), (0,)))
    square.scatter()
    open_ref[...] = opened
    early.collect()
    early_ref[...] = early.totals[...]
    square.over_y()
    image.over_y()
    square.over_last()
    image.over_last()
    image.back()
    square.back()
    image.collect()
    square.collect()
    late_ref[0:T] = image.totals[...]
    late_ref[T : 2 * T] = square.totals[...]

    for c in pending:
        c.wait_send()


def sum_scratch(rows, group, last):
    size = rows // group
    counts = (group, NY, last)
    sems = [pltpu.SemaphoreType.DMA((n,)) for n in counts + (group,)]
    return (
        [pltpu.VMEM((rows, T), F32)] * 2
        + [pltpu.VMEM((n, size, T), F32) for n in counts]
        + [pltpu.VMEM((size, T), F32)] * 3
        + sems * 2
    )


def communicate(rows, cols, count, v, vp, coupling, tiles):
    vmem = pl.BlockSpec(memory_space=pltpu.VMEM)
    smem = pl.BlockSpec(memory_space=pltpu.SMEM)
    dma = pltpu.SemaphoreType.DMA
    pair = (2, 4, 2, T, T)
    return pl.pallas_call(
        step_kernel,
        out_shape=(
            jax.ShapeDtypeStruct((2 * T, T), F32),
            jax.ShapeDtypeStruct((2 * T, T), F32),
            jax.ShapeDtypeStruct((2 * T, T), F32),
        ),
        in_specs=[smem, smem, smem] + [pl.BlockSpec(memory_space=pl.ANY)] * 4,
        out_specs=(vmem, vmem, vmem),
        scratch_shapes=[
            pltpu.VMEM((2 * T, T), F32),
            pltpu.VMEM((2 * T, T), F32),
            pltpu.VMEM((T, T), F32),
            pltpu.VMEM((SLOTS, T, T), BF16),
            dma((4,)),
            pltpu.SMEM((NX * NZ * 2,), jnp.int32),
            pltpu.SMEM((SLOTS,), jnp.int32),
            pltpu.VMEM((2, T, T), BF16),
            pltpu.VMEM((2 * SLOTS, T, T), BF16),
            pltpu.VMEM((SLOTS + 1, T, T), F32),
            pltpu.VMEM((SLOTS + 1, T, T), BF16),
            pltpu.VMEM((2 * T, T), F32),
            pltpu.VMEM((T, 2 * T), F32),
        ]
        + [pltpu.VMEM(pair, BF16)] * 6
        + [
            pltpu.VMEM((2, T, T), F32),
            pltpu.VMEM(pair, BF16),
            pltpu.VMEM(pair, BF16),
            pltpu.VMEM((2, T, T), BF16),
            pltpu.VMEM((2, T, T), BF16),
            dma((2, 4, 2)), dma((2, 4, 2)), dma((NY, 2)), dma((NY, 2)),
            dma((3, 2, 4)), dma((3, 2, 4)), dma((2, 4)), dma((2, 4)), dma((2,)), dma((2,)),
        ]
        + sum_scratch(T, NZ * NC, NX)
        + sum_scratch(T, NX * NC, NZ)
        + sum_scratch(2 * T, NZ * NC, NX),
        compiler_params=pltpu.CompilerParams(collective_id=0, has_side_effects=True),
        name="krylov_step",
    )(rows, cols, count, v, vp, coupling, tiles)


def factor_kernel(total, late_ref, early_ref, open_ref, v_ref, basis_ref, projection_ref, rfactor_ref, residual, inverse_ref):
    image = late_ref[0:T]
    along = image * (1.0 / total)
    projection_ref[...] = image * total ** (-0.5)
    residual[...] = open_ref[...] - dot(v_ref[...], along, ((1,), (0,)))
    inner = (image - early_ref[T : 2 * T]) * (1.0 / total)
    inner = inner - 0.5 * dot(early_ref[0:T] * (1.0 / total), along, ((1,), (0,)))
    cross = dot(along, inner, ((0,), (0,)))
    gram = late_ref[T : 2 * T] * (1.0 / total) - cross - cross.T
    lane = lax.broadcasted_iota(jnp.int32, (1, T), 1)
    groups = T // 8
    left = [gram[8 * i : 8 * i + 8] for i in range(groups)]
    sub8 = lax.broadcasted_iota(jnp.int32, (8, T), 0)
    lane8 = lax.broadcasted_iota(jnp.int32, (8, T), 1)
    right = [jnp.where(lane8 == sub8 + 8 * i, 1.0, 0.0).astype(F32) for i in range(groups)]

    def spread(row):
        return jnp.broadcast_to(row, (8, T))

    for p in range(groups):
        panel, other = left[p], right[p]
        columns = [jnp.broadcast_to(panel[:, 8 * p + j : 8 * p + j + 1], (8, T)) for j in range(8)]
        a = [[spread(columns[j][i : i + 1]) for j in range(i + 1)] for i in range(8)]
        inv = [[None] * 8 for _ in range(8)]
        low = [[None] * 8 for _ in range(8)]
        for j in range(8):
            inv[j][j] = lax.rsqrt(a[j][j])
            for i in range(j + 1, 8):
                low[i][j] = a[i][j] * inv[j][j]
            for i in range(j + 1, 8):
                for k in range(j + 1, i + 1):
                    a[i][k] = a[i][k] - low[i][j] * low[k][j]
            for k in range(j):
                s = low[j][k] * inv[k][k]
                for m in range(k + 1, j):
                    s = s + low[j][m] * inv[m][k]
                inv[j][k] = -(s * inv[j][j])
        rows_l = [spread(panel[j : j + 1]) for j in range(8)]
        rows_r = [spread(other[j : j + 1]) for j in range(8)]

        def mix(rows, weight, picks):
            value = None
            for j in picks:
                term = weight(j) * rows[j]
                value = term if value is None else value + term
            return value

        out_l = [mix(rows_l, lambda j, i=i: inv[i][j], range(i + 1)) for i in range(8)]
        out_r = [mix(rows_r, lambda j, i=i: inv[i][j], range(i + 1)) for i in range(8)]
        for i in range(8):
            r = 8 * p + i
            rfactor_ref[pl.ds(r, 1)] = jnp.where(lane >= r, out_l[i][0:1], 0.0)
            inverse_ref[pl.ds(r, 1)] = out_r[i][0:1]
        if p + 1 < groups:
            back_l = [mix(out_l, lambda i, j=j: inv[i][j], range(j, 8)) for j in range(8)]
            back_r = [mix(out_r, lambda i, j=j: inv[i][j], range(j, 8)) for j in range(8)]
            for g in range(p + 1, groups):
                cols = [jnp.broadcast_to(left[g][:, 8 * p + j : 8 * p + j + 1], (8, T)) for j in range(8)]
                left[g] = left[g] - mix(back_l, lambda j: cols[j], range(8))
                right[g] = right[g] - mix(back_r, lambda j: cols[j], range(8))
    basis_ref[...] = dot(residual[...], inverse_ref[...], ((1,), (1,)))


def factor(total, late, early, opened, v):
    vmem = pl.BlockSpec(memory_space=pltpu.VMEM)
    return pl.pallas_call(
        functools.partial(factor_kernel, total),
        out_shape=(
            jax.ShapeDtypeStruct((2 * T, T), F32),
            jax.ShapeDtypeStruct((T, T), F32),
            jax.ShapeDtypeStruct((T, T), F32),
        ),
        in_specs=[vmem] * 4,
        out_specs=(vmem,) * 3,
        scratch_shapes=[pltpu.VMEM((2 * T, T), F32), pltpu.VMEM((T, T), F32)],
        name="factor",
    )(late, early, opened, v)


def on_device(basis_now, basis_prev, coupling, tiles, tile_rows, tile_cols, tile_counts):
    opened, late, early = communicate(
        tile_rows[0, 0], tile_cols[0, 0], tile_counts[0], basis_now, basis_prev, coupling, tiles[0, 0]
    )
    total = float(NX * NZ * NY * NC * 2 * T)
    return factor(total, late, early, opened, basis_now)


def solution(mesh):
    placed = (
        P(("row", "col"), None),
        P(("row", "col"), None),
        P(),
        P("row", "col", None, None, None),
        P("row", "col", None),
        P("row", "col", None),
        P("row", "col"),
    )
    return jax.shard_map(
        on_device,
        mesh=mesh,
        in_specs=placed,
        out_specs=(P(("row", "col"), None), P(), P()),
        check_vma=False,
    )
```

```python
import functools

import jax
import jax.numpy as jnp
from jax import lax
from jax.experimental import pallas as pl
from jax.experimental.pallas import tpu as pltpu
from jax.sharding import PartitionSpec as P

HIGHEST = lax.Precision.HIGHEST
MESH = pl.DeviceIdType.MESH
F32 = jnp.float32
BF16 = jnp.bfloat16

NX, NZ, NY, NC = 4, 8, 8, 2
SLOTS = 16
T = 128
AHEAD = (4, 3, 2, 1)
BEHIND = (0, -3, -2, -1)


def dot(a, b, dims):
    return lax.dot_general(a, b, (dims, ((), ())), precision=HIGHEST, preferred_element_type=F32)


def step_kernel(
    rows_ref, cols_ref, count_ref, v_ref, vp_ref, coupling_ref, tiles_ref,
    open_ref, late_ref, early_ref,
    v_s, vp_s, coupling_s, tiles_s, local_sem,
    latest, before, half, gathered, sums, sums16, prev_part, vt,
    fwd, direct, comb, fwd_in, direct_in, comb_in,
    own, zsend, zrecv, zhalf, zhalf_in,
    ring_s, ring_r, pair_s, pair_r, x_s, x_r, z_s, z_r, zh_s, zh_r,
    *sum_refs,
):
    row = lax.axis_index("row")
    col = lax.axis_index("col")
    x, z = row // NZ, row % NZ
    y, core = col // NC, col % NC

    def at(dx=0, dz=0, dy=0, dc=0):
        return (
            ((x + dx + NX) % NX) * NZ + (z + dz + NZ) % NZ,
            ((y + dy + NY) % NY) * NC + (core + dc) % NC,
        )

    def copy(src, dst, send, recv, device):
        return pltpu.make_async_remote_copy(
            src_ref=src, dst_ref=dst, send_sem=send, recv_sem=recv, device_id=device, device_id_type=MESH
        )

    barrier = pltpu.get_barrier_semaphore()
    peers = [at(dz=d // 2, dc=d % 2) for d in range(1, 16)]
    peers += [at(dy=d) for d in range(1, NY)] + [at(dx=d, dc=c) for d in range(1, NX) for c in range(2)]
    for peer in peers:
        pl.semaphore_signal(barrier, inc=1, device_id=peer, device_id_type=MESH)

    loads = [
        pltpu.make_async_copy(src, dst, local_sem.at[i])
        for i, (src, dst) in enumerate(
            ((v_ref, v_s), (vp_ref, vp_s), (coupling_ref, coupling_s), (tiles_ref, tiles_s))
        )
    ]
    for load in loads:
        load.start()
    loads[0].wait()
    half[...] = v_s[...].astype(BF16).reshape(2, T, T)
    pl.semaphore_wait(barrier, len(peers))

    def start(c):
        c.start()

    def sent(ref, sem):
        copy(ref, ref, sem, sem, at(dc=1)).wait_send()

    def block(origin, h, c):
        return gathered.at[2 * (NC * origin + c) + h]

    def along(direction, far, h):
        d = 0 if direction == 1 else 1
        if far <= 2:
            src, dst, device = half.at[h], block(y, h, core), at(dy=far * direction)
        else:
            dst = block((y - 2 * direction + NY) % NY, h, core)
            src, device = dst, at(dy=(far - 2) * direction)
        return copy(src, dst, ring_s.at[0], ring_r.at[d, far - 1, h], device)

    def arrived(direction, far, h):
        d = 0 if direction == 1 else 1
        dst = block((y - direction * far + NY) % NY, h, core)
        return copy(dst, dst, ring_s.at[0], ring_r.at[d, far - 1, h], at(dy=direction))

    def to_pair(delta, h):
        origin = (y + delta + NY) % NY
        dst = block(origin, h, core)
        src = half.at[h] if delta == 0 else dst
        return copy(src, dst, pair_s.at[0], pair_r.at[0], at(dc=1))

    def has(direction, far, h):
        return far < 4 or (h == 0) == (direction == 1)

    for far in (2, 1):
        for h in range(2):
            for direction in (1, -1):
                start(along(direction, far, h))
    for h in range(2):
        start(to_pair(0, h))

    class Sum:
        def __init__(self, refs, over_z):
            self.part, self.totals, self.red, self.piece, self.send, self.recv = (
                refs[0], refs[1], refs[2:5], refs[5:8], refs[8], refs[9]
            )
            self.over_z = over_z
            self.place = (z if over_z else x) * NC + core
            self.last = x if over_z else z
            self.group, self.size, _ = self.red[0].shape

        def member(self, d):
            h = (self.place + d) % self.group
            if self.over_z:
                return h, (x * NZ + h // NC, y * NC + h % NC)
            return h, ((h // NC) * NZ + z, y * NC + h % NC)

        def rows(self, ref, h):
            return ref.at[pl.ds(self.size * h, self.size)]

        def move(self, stage, src, dst, device):
            return copy(src, dst, self.send.at[stage], self.recv.at[stage], device)

        def others(self, stage):
            if stage == 3:
                return self.totals.at[pl.ds(0, self.size * (self.group - 1))]
            return self.red[stage].at[pl.ds(0, self.red[stage].shape[0] - 1)]

        def wait(self, stage):
            self.move(stage, self.others(stage), self.others(stage), at(dc=1)).wait_recv()

        def drain(self, stages):
            for stage in stages:
                self.move(stage, self.others(stage), self.others(stage), at(dc=1)).wait_send()

        def scatter(self):
            for d in range(1, self.group):
                h, device = self.member(d)
                start(self.move(0, self.rows(self.part, h), self.red[0].at[self.place], device))
            self.red[0][self.place] = self.part[pl.ds(self.size * self.place, self.size)]

        def reduce(self, stage):
            self.wait(stage)
            self.piece[stage][...] = jnp.sum(self.red[stage][...], axis=0)
            return self.piece[stage]

        def spread(self, stage, piece, i, device_at):
            red = self.red[stage]
            for d in range(1, red.shape[0]):
                start(self.move(stage, piece, red.at[i], device_at(d)))
            red[i] = piece[...]

        def over_y(self):
            self.spread(1, self.reduce(0), y, lambda d: at(dy=d))

        def over_last(self):
            piece = self.reduce(1)
            self.spread(2, piece, self.last, (lambda d: at(dx=d)) if self.over_z else (lambda d: at(dz=d)))

        def back(self):
            piece = self.reduce(2)
            for d in range(1, self.group):
                h, device = self.member(d)
                start(self.move(3, piece, self.rows(self.totals, self.place), device))
            self.totals[pl.ds(self.size * self.place, self.size)] = piece[...]

        def collect(self):
            self.wait(3)

    image, square, early = (Sum(sum_refs[10 * i : 10 * i + 10], over_z) for i, over_z in enumerate((True, False, True)))

    def take(far):
        for h in range(2):
            for direction in (1, -1):
                if has(direction, far, h):
                    arrived(direction, far, h).wait_recv()
                    if far == 2:
                        start(along(direction, 3, h))
                        if has(direction, 4, h):
                            start(along(direction, 4, h))
                    start(to_pair(-direction * far, h))

    gathered[pl.ds(2 * col, 2)] = half[...]
    loads[1].wait()
    loads[2].wait()
    i0 = lax.broadcasted_iota(jnp.int32, (T, T), 0)
    i1 = lax.broadcasted_iota(jnp.int32, (T, T), 1)
    upper = jnp.where(i0 <= i1, coupling_s[...], 0.0)
    prev_part[...] = dot(vp_s[...], upper, ((1,), (1,)))
    vt[...] = v_s[...].T
    early.part[0:T] = dot(vt[...], v_s[...], ((1,), (0,)))
    early.part[T : 2 * T] = dot(vt[...], prev_part[...], ((1,), (0,)))
    early.scatter()
    take(2)
    take(1)

    sums[SLOTS] = jnp.zeros((T, T), F32)
    sums16[SLOTS] = jnp.zeros((T, T), BF16)
    count = count_ref[0]
    used = [jnp.where(t < count, rows_ref[t], -1) for t in range(SLOTS)]

    def find(r, carry):
        found = jnp.int32(SLOTS)
        for t in range(SLOTS):
            found = jnp.where(used[t] == r, t, found)
        latest[r] = found
        return carry

    lax.fori_loop(0, NX * NZ * 2, find, 0)
    for t in range(SLOTS):
        found = jnp.int32(SLOTS)
        for s in range(t):
            found = jnp.where(used[s] == used[t], s, found)
        before[t] = found
    loads[3].wait()
    early.over_y()
    take(3)
    take(4)
    others = gathered.at[pl.ds(0, SLOTS)]
    copy(others, others, pair_s.at[0], pair_r.at[0], at(dc=1)).wait_recv()

    for t in range(SLOTS):
        value = sums[before[t]] + jnp.dot(tiles_s[t], gathered[cols_ref[t]], preferred_element_type=F32)
        sums[t] = value
        sums16[t] = value.astype(BF16)

    def tile_of(dx, dz, h):
        return 2 * (((x + dx + NX) % NX) * NZ + (z + dz + NZ) % NZ) + h

    def fill(dst, dx, dz):
        for h in range(2):
            dst[h] = sums16[latest[tile_of(dx, dz, h)]]

    def xcopy(kind, s, k):
        src = (fwd, direct, comb)[kind].at[s, k]
        dst = (fwd_in, direct_in, comb_in)[kind].at[s, k]
        return copy(src, dst, x_s.at[kind], x_r.at[kind, s, k], at(dx=1 if s == 0 else -1))

    side = (AHEAD, BEHIND)

    def send_forward(k):
        for s in range(2):
            fill(fwd.at[s, k], 2, side[s][k])
            start(xcopy(0, s, k))

    def send_direct(k):
        for s in range(2):
            fill(direct.at[s, k], 1 if s == 0 else -1, side[1 - s][k])
            start(xcopy(1, s, k))

    def send_combined(k):
        for s in range(2):
            xcopy(0, s, k).wait_recv()
            for h in range(2):
                mine = sums[latest[tile_of(1 if s == 0 else -1, side[s][k], h)]]
                comb[s, k, h] = (mine + fwd_in[s, k, h].astype(F32)).astype(BF16)
            start(xcopy(2, s, k))

    def zcopy(s, k):
        return copy(zsend.at[4 * s + k], zrecv.at[s, k], z_s.at[0], z_r.at[s, k], at(dz=side[s][k]))

    def zhalf_copy(s):
        return copy(zhalf.at[s], zhalf_in.at[s], zh_s.at[0], zh_r.at[s], at(dz=1 if s == 0 else -1))

    def line_sum(s, k, h):
        mine = sums[latest[tile_of(0, side[s][k], h)]]
        return mine + comb_in[s, k, h].astype(F32) + direct_in[1 - s, k, h].astype(F32)

    def finish(k):
        for s in range(2):
            xcopy(2, s, k).wait_recv()
            xcopy(1, 1 - s, k).wait_recv()
            if k == 1:
                zhalf_copy(s).wait_recv()
            for h in range(2):
                value = line_sum(s, k, h)
                if k == 0 and s == 0:
                    zhalf[h] = value.astype(BF16)
                    start(zhalf_copy(h))
                elif k == 0:
                    own[h] = value
                else:
                    if k == 1 and h == s:
                        value = value + zhalf_in[s].astype(F32)
                    zsend[4 * s + k, h] = value.astype(BF16)
            if k > 0:
                start(zcopy(s, k))

    send_forward(0)
    send_forward(1)
    send_direct(0)
    send_forward(2)
    early.over_last()
    send_combined(0)
    send_direct(1)
    send_forward(3)
    send_combined(1)
    early.back()
    send_direct(2)
    finish(0)
    send_combined(2)
    send_direct(3)
    finish(1)
    send_combined(3)
    finish(2)
    finish(3)
    product = own[...]
    for k in range(1, 4):
        for s in range(2):
            zcopy(s, k).wait_recv()
            product = product + zrecv[s, k].astype(F32)
    product = product.reshape(2 * T, T)

    opened = product - prev_part[...]
    image.part[...] = dot(vt[...], product, ((1,), (0,)))
    image.scatter()
    square.part[...] = dot(opened, opened, ((0,), (0,)))
    square.scatter()
    open_ref[...] = opened
    sent(gathered.at[pl.ds(0, 14)], ring_s.at[0])
    sent(others, pair_s.at[0])
    for kind, ref in enumerate((fwd, direct, comb)):
        sent(ref, x_s.at[kind])
    sent(zsend.at[pl.ds(0, 6)], z_s.at[0])
    sent(zhalf, zh_s.at[0])
    early.collect()
    early.drain(range(4))
    early_ref[...] = early.totals[...]
    square.over_y()
    image.over_y()
    square.over_last()
    image.over_last()
    image.back()
    square.back()
    image.drain(range(3))
    square.drain(range(3))
    image.collect()
    square.collect()
    late_ref[0:T] = image.totals[...]
    late_ref[T : 2 * T] = square.totals[...]

    image.drain((3,))
    square.drain((3,))


def sum_scratch(rows, group, last):
    size = rows // group
    counts = (group, NY, last)
    return (
        [pltpu.VMEM((rows, T), F32)] * 2
        + [pltpu.VMEM((n, size, T), F32) for n in counts]
        + [pltpu.VMEM((size, T), F32)] * 3
        + [pltpu.SemaphoreType.DMA((4,))] * 2
    )


def communicate(rows, cols, count, v, vp, coupling, tiles):
    vmem = pl.BlockSpec(memory_space=pltpu.VMEM)
    smem = pl.BlockSpec(memory_space=pltpu.SMEM)
    dma = pltpu.SemaphoreType.DMA
    pair = (2, 4, 2, T, T)
    return pl.pallas_call(
        step_kernel,
        out_shape=(
            jax.ShapeDtypeStruct((2 * T, T), F32),
            jax.ShapeDtypeStruct((2 * T, T), F32),
            jax.ShapeDtypeStruct((2 * T, T), F32),
        ),
        in_specs=[smem, smem, smem] + [pl.BlockSpec(memory_space=pl.ANY)] * 4,
        out_specs=(vmem, vmem, vmem),
        scratch_shapes=[
            pltpu.VMEM((2 * T, T), F32),
            pltpu.VMEM((2 * T, T), F32),
            pltpu.VMEM((T, T), F32),
            pltpu.VMEM((SLOTS, T, T), BF16),
            dma((4,)),
            pltpu.SMEM((NX * NZ * 2,), jnp.int32),
            pltpu.SMEM((SLOTS,), jnp.int32),
            pltpu.VMEM((2, T, T), BF16),
            pltpu.VMEM((2 * SLOTS, T, T), BF16),
            pltpu.VMEM((SLOTS + 1, T, T), F32),
            pltpu.VMEM((SLOTS + 1, T, T), BF16),
            pltpu.VMEM((2 * T, T), F32),
            pltpu.VMEM((T, 2 * T), F32),
        ]
        + [pltpu.VMEM(pair, BF16)] * 6
        + [
            pltpu.VMEM((2, T, T), F32),
            pltpu.VMEM((8, 2, T, T), BF16),
            pltpu.VMEM(pair, BF16),
            pltpu.VMEM((2, T, T), BF16),
            pltpu.VMEM((2, T, T), BF16),
            dma((1,)), dma((2, 4, 2)), dma((1,)), dma((1,)),
            dma((3,)), dma((3, 2, 4)), dma((1,)), dma((2, 4)), dma((1,)), dma((2,)),
        ]
        + sum_scratch(T, NZ * NC, NX)
        + sum_scratch(T, NX * NC, NZ)
        + sum_scratch(2 * T, NZ * NC, NX),
        compiler_params=pltpu.CompilerParams(collective_id=0, has_side_effects=True),
        name="krylov_step",
    )(rows, cols, count, v, vp, coupling, tiles)


def factor_kernel(total, late_ref, early_ref, open_ref, v_ref, basis_ref, projection_ref, rfactor_ref, residual, inverse_ref):
    image = late_ref[0:T]
    along = image * (1.0 / total)
    projection_ref[...] = image * total ** (-0.5)
    residual[...] = open_ref[...] - dot(v_ref[...], along, ((1,), (0,)))
    inner = (image - early_ref[T : 2 * T]) * (1.0 / total)
    inner = inner - 0.5 * dot(early_ref[0:T] * (1.0 / total), along, ((1,), (0,)))
    cross = dot(along, inner, ((0,), (0,)))
    gram = late_ref[T : 2 * T] * (1.0 / total) - cross - cross.T
    lane = lax.broadcasted_iota(jnp.int32, (1, T), 1)
    groups = T // 8
    left = [gram[8 * i : 8 * i + 8] for i in range(groups)]
    sub8 = lax.broadcasted_iota(jnp.int32, (8, T), 0)
    lane8 = lax.broadcasted_iota(jnp.int32, (8, T), 1)
    right = [jnp.where(lane8 == sub8 + 8 * i, 1.0, 0.0).astype(F32) for i in range(groups)]

    def spread(row):
        return jnp.broadcast_to(row, (8, T))

    def mix(rows, weight):
        value = None
        for j in range(8):
            term = weight[j] * rows[j]
            value = term if value is None else value + term
        return value

    for p in range(groups):
        panel, other = left[p], right[p]
        columns = [jnp.broadcast_to(panel[:, 8 * p + j : 8 * p + j + 1], (8, T)) for j in range(8)]
        a = [[spread(columns[j][i : i + 1]) for j in range(i + 1)] for i in range(8)]
        low = [[None] * 8 for _ in range(8)]
        inv = [None] * 8
        rows_l = [spread(panel[j : j + 1]) for j in range(8)]
        rows_r = [spread(other[j : j + 1]) for j in range(8)]
        for j in range(8):
            inv[j] = lax.rsqrt(a[j][j])
            for i in range(j + 1, 8):
                low[i][j] = a[i][j] * inv[j]
            for i in range(j + 1, 8):
                for k in range(j + 1, i + 1):
                    a[i][k] = a[i][k] - low[i][j] * low[k][j]
            rows_l[j] = rows_l[j] * inv[j]
            rows_r[j] = rows_r[j] * inv[j]
            for i in range(j + 1, 8):
                rows_l[i] = rows_l[i] - low[i][j] * rows_l[j]
                rows_r[i] = rows_r[i] - low[i][j] * rows_r[j]
        for i in range(8):
            r = 8 * p + i
            rfactor_ref[pl.ds(r, 1)] = jnp.where(lane >= r, rows_l[i][0:1], 0.0)
            inverse_ref[pl.ds(r, 1)] = rows_r[i][0:1]
        if p + 1 < groups:
            back_l, back_r = [None] * 8, [None] * 8
            for j in range(7, -1, -1):
                sum_l, sum_r = rows_l[j], rows_r[j]
                for i in range(j + 1, 8):
                    sum_l = sum_l - low[i][j] * back_l[i]
                    sum_r = sum_r - low[i][j] * back_r[i]
                back_l[j] = sum_l * inv[j]
                back_r[j] = sum_r * inv[j]
            for g in range(p + 1, groups):
                cols = [jnp.broadcast_to(left[g][:, 8 * p + j : 8 * p + j + 1], (8, T)) for j in range(8)]
                left[g] = left[g] - mix(back_l, cols)
                right[g] = right[g] - mix(back_r, cols)
    basis_ref[...] = dot(residual[...], inverse_ref[...], ((1,), (1,)))


def factor(total, late, early, opened, v):
    vmem = pl.BlockSpec(memory_space=pltpu.VMEM)
    return pl.pallas_call(
        functools.partial(factor_kernel, total),
        out_shape=(
            jax.ShapeDtypeStruct((2 * T, T), F32),
            jax.ShapeDtypeStruct((T, T), F32),
            jax.ShapeDtypeStruct((T, T), F32),
        ),
        in_specs=[vmem] * 4,
        out_specs=(vmem,) * 3,
        scratch_shapes=[pltpu.VMEM((2 * T, T), F32), pltpu.VMEM((T, T), F32)],
        name="factor",
    )(late, early, opened, v)


def on_device(basis_now, basis_prev, coupling, tiles, tile_rows, tile_cols, tile_counts):
    opened, late, early = communicate(
        tile_rows[0, 0], tile_cols[0, 0], tile_counts[0], basis_now, basis_prev, coupling, tiles[0, 0]
    )
    total = float(NX * NZ * NY * NC * 2 * T)
    return factor(total, late, early, opened, basis_now)


def solution(mesh):
    placed = (
        P(("row", "col"), None),
        P(("row", "col"), None),
        P(),
        P("row", "col", None, None, None),
        P("row", "col", None),
        P("row", "col", None),
        P("row", "col"),
    )
    return jax.shard_map(
        on_device,
        mesh=mesh,
        in_specs=placed,
        out_specs=(P(("row", "col"), None), P(), P()),
        check_vma=False,
    )
```

```python
import functools

import jax
import jax.numpy as jnp
from jax import lax
from jax.experimental import pallas as pl
from jax.experimental.pallas import tpu as pltpu
from jax.sharding import PartitionSpec as P

HIGHEST = lax.Precision.HIGHEST
MESH = pl.DeviceIdType.MESH
F32 = jnp.float32
BF16 = jnp.bfloat16

NX, NZ, NY, NC = 4, 8, 8, 2
SLOTS = 16
T = 128
AHEAD = (4, 3, 2, 1)
BEHIND = (0, -3, -2, -1)


def dot(a, b, dims):
    return lax.dot_general(a, b, (dims, ((), ())), precision=HIGHEST, preferred_element_type=F32)


def step_kernel(
    rows_in, cols_in, count_in, v_ref, vp_ref, coupling_ref, tiles_ref,
    open_ref, late_ref, early_ref,
    rows_ref, cols_ref, count_ref, v_s, vp_s, coupling_s, tiles_s, local_sem,
    latest, before, half, gathered, sums, sums16, prev_part, vt,
    fwd, direct, comb, fwd_in, direct_in, comb_in,
    own, zsend, zrecv, zhalf, zhalf_in,
    ring_s, ring_r, pair_s, pair_r, x_s, x_r, z_s, z_r, zh_s, zh_r,
    *sum_refs,
):
    row = lax.axis_index("row")
    col = lax.axis_index("col")
    x, z = row // NZ, row % NZ
    y, core = col // NC, col % NC

    def at(dx=0, dz=0, dy=0, dc=0):
        return (
            ((x + dx + NX) % NX) * NZ + (z + dz + NZ) % NZ,
            ((y + dy + NY) % NY) * NC + (core + dc) % NC,
        )

    def copy(src, dst, send, recv, device):
        return pltpu.make_async_remote_copy(
            src_ref=src, dst_ref=dst, send_sem=send, recv_sem=recv, device_id=device, device_id_type=MESH
        )

    loads = [
        pltpu.make_async_copy(src, dst, local_sem.at[i])
        for i, (src, dst) in enumerate(
            (
                (v_ref, v_s), (vp_ref, vp_s), (coupling_ref, coupling_s), (tiles_ref, tiles_s),
                (rows_in, rows_ref), (cols_in, cols_ref), (count_in, count_ref),
            )
        )
    ]
    for load in loads:
        load.start()
    barrier = pltpu.get_barrier_semaphore()
    peers = [at(dy=d) for d in range(1, NY)] + [at(dz=d // 2, dc=d % 2) for d in range(1, 16)]
    peers += [at(dx=d, dc=c) for d in range(1, NX) for c in range(2)]
    for peer in peers:
        pl.semaphore_signal(barrier, inc=1, device_id=peer, device_id_type=MESH)

    loads[0].wait()
    half[...] = v_s[...].astype(BF16).reshape(2, T, T)
    pl.semaphore_wait(barrier, len(peers))

    def start(c):
        c.start()

    def sent(ref, sem):
        copy(ref, ref, sem, sem, at(dc=1)).wait_send()

    def block(origin, h, c):
        return gathered.at[2 * (NC * origin + c) + h]

    def along(direction, far, h):
        d = 0 if direction == 1 else 1
        if far <= 2:
            src, dst, device = half.at[h], block(y, h, core), at(dy=far * direction)
        else:
            dst = block((y - 2 * direction + NY) % NY, h, core)
            src, device = dst, at(dy=(far - 2) * direction)
        return copy(src, dst, ring_s.at[0], ring_r.at[d, far - 1, h], device)

    def arrived(direction, far, h):
        d = 0 if direction == 1 else 1
        dst = block((y - direction * far + NY) % NY, h, core)
        return copy(dst, dst, ring_s.at[0], ring_r.at[d, far - 1, h], at(dy=direction))

    def to_pair(delta, h):
        origin = (y + delta + NY) % NY
        dst = block(origin, h, core)
        src = half.at[h] if delta == 0 else dst
        return copy(src, dst, pair_s.at[0], pair_r.at[0], at(dc=1))

    def has(direction, far, h):
        return far < 4 or (h == 0) == (direction == 1)

    for far in (2, 1):
        for h in range(2):
            for direction in (1, -1):
                start(along(direction, far, h))
    for h in range(2):
        start(to_pair(0, h))

    class Sum:
        def __init__(self, refs, over_z):
            self.part, self.totals, self.red, self.piece, self.send, self.recv = (
                refs[0], refs[1], refs[2:5], refs[5:8], refs[8], refs[9]
            )
            self.over_z = over_z
            self.place = (z if over_z else x) * NC + core
            self.last = x if over_z else z
            self.group, self.size, _ = self.red[0].shape

        def member(self, d):
            h = (self.place + d) % self.group
            if self.over_z:
                return h, (x * NZ + h // NC, y * NC + h % NC)
            return h, ((h // NC) * NZ + z, y * NC + h % NC)

        def rows(self, ref, h):
            return ref.at[pl.ds(self.size * h, self.size)]

        def move(self, stage, src, dst, device):
            return copy(src, dst, self.send.at[stage], self.recv.at[stage], device)

        def others(self, stage):
            if stage == 3:
                return self.totals.at[pl.ds(0, self.size * (self.group - 1))]
            return self.red[stage].at[pl.ds(0, self.red[stage].shape[0] - 1)]

        def wait(self, stage):
            self.move(stage, self.others(stage), self.others(stage), at(dc=1)).wait_recv()

        def drain(self, stages):
            for stage in stages:
                self.move(stage, self.others(stage), self.others(stage), at(dc=1)).wait_send()

        def scatter(self):
            for d in range(1, self.group):
                h, device = self.member(d)
                start(self.move(0, self.rows(self.part, h), self.red[0].at[self.place], device))
            self.red[0][self.place] = self.part[pl.ds(self.size * self.place, self.size)]

        def reduce(self, stage):
            self.wait(stage)
            self.piece[stage][...] = jnp.sum(self.red[stage][...], axis=0)
            return self.piece[stage]

        def spread(self, stage, piece, i, device_at):
            red = self.red[stage]
            for d in range(1, red.shape[0]):
                start(self.move(stage, piece, red.at[i], device_at(d)))
            red[i] = piece[...]

        def over_y(self):
            self.spread(1, self.reduce(0), y, lambda d: at(dy=d))

        def over_last(self):
            piece = self.reduce(1)
            self.spread(2, piece, self.last, (lambda d: at(dx=d)) if self.over_z else (lambda d: at(dz=d)))

        def back(self):
            piece = self.reduce(2)
            for d in range(1, self.group):
                h, device = self.member(d)
                start(self.move(3, piece, self.rows(self.totals, self.place), device))
            self.totals[pl.ds(self.size * self.place, self.size)] = piece[...]

        def collect(self):
            self.wait(3)

    image, square, early = (Sum(sum_refs[10 * i : 10 * i + 10], over_z) for i, over_z in enumerate((True, False, True)))

    def take(far):
        for h in range(2):
            for direction in (1, -1):
                if has(direction, far, h):
                    arrived(direction, far, h).wait_recv()
                    if far == 2:
                        start(along(direction, 3, h))
                        if has(direction, 4, h):
                            start(along(direction, 4, h))
                    start(to_pair(-direction * far, h))

    gathered[pl.ds(2 * col, 2)] = half[...]
    loads[1].wait()
    loads[2].wait()
    i0 = lax.broadcasted_iota(jnp.int32, (T, T), 0)
    i1 = lax.broadcasted_iota(jnp.int32, (T, T), 1)
    upper = jnp.where(i0 <= i1, coupling_s[...], 0.0)
    prev_part[...] = dot(vp_s[...], upper, ((1,), (1,)))
    vt[...] = v_s[...].T
    early.part[0:T] = dot(vt[...], v_s[...], ((1,), (0,)))
    early.part[T : 2 * T] = dot(vt[...], prev_part[...], ((1,), (0,)))
    early.scatter()
    take(2)
    take(1)

    sums[SLOTS] = jnp.zeros((T, T), F32)
    sums16[SLOTS] = jnp.zeros((T, T), BF16)
    for load in loads[4:]:
        load.wait()
    count = count_ref[0]
    used = [jnp.where(t < count, rows_ref[t], -1) for t in range(SLOTS)]

    def find(r, carry):
        found = jnp.int32(SLOTS)
        for t in range(SLOTS):
            found = jnp.where(used[t] == r, t, found)
        latest[r] = found
        return carry

    lax.fori_loop(0, NX * NZ * 2, find, 0)
    for t in range(SLOTS):
        found = jnp.int32(SLOTS)
        for s in range(t):
            found = jnp.where(used[s] == used[t], s, found)
        before[t] = found
    loads[3].wait()
    early.over_y()
    take(3)
    take(4)
    others = gathered.at[pl.ds(0, SLOTS)]
    copy(others, others, pair_s.at[0], pair_r.at[0], at(dc=1)).wait_recv()

    for t in range(SLOTS):
        value = sums[before[t]] + jnp.dot(tiles_s[t], gathered[cols_ref[t]], preferred_element_type=F32)
        sums[t] = value
        sums16[t] = value.astype(BF16)

    def tile_of(dx, dz, h):
        return 2 * (((x + dx + NX) % NX) * NZ + (z + dz + NZ) % NZ) + h

    def fill(dst, dx, dz):
        for h in range(2):
            dst[h] = sums16[latest[tile_of(dx, dz, h)]]

    def xcopy(kind, s, k):
        src = (fwd, direct, comb)[kind].at[s, k]
        dst = (fwd_in, direct_in, comb_in)[kind].at[s, k]
        return copy(src, dst, x_s.at[kind], x_r.at[kind, s, k], at(dx=1 if s == 0 else -1))

    side = (AHEAD, BEHIND)

    def send_forward(k):
        for s in range(2):
            fill(fwd.at[s, k], 2, side[s][k])
            start(xcopy(0, s, k))

    def send_direct(k):
        for s in range(2):
            fill(direct.at[s, k], 1 if s == 0 else -1, side[1 - s][k])
            start(xcopy(1, s, k))

    def send_combined(k):
        for s in range(2):
            xcopy(0, s, k).wait_recv()
            for h in range(2):
                mine = sums[latest[tile_of(1 if s == 0 else -1, side[s][k], h)]]
                comb[s, k, h] = (mine + fwd_in[s, k, h].astype(F32)).astype(BF16)
            start(xcopy(2, s, k))

    def zcopy(s, k):
        return copy(zsend.at[4 * s + k], zrecv.at[s, k], z_s.at[0], z_r.at[s, k], at(dz=side[s][k]))

    def zhalf_copy(s):
        return copy(zhalf.at[s], zhalf_in.at[s], zh_s.at[0], zh_r.at[s], at(dz=1 if s == 0 else -1))

    def line_sum(s, k, h):
        mine = sums[latest[tile_of(0, side[s][k], h)]]
        return mine + comb_in[s, k, h].astype(F32) + direct_in[1 - s, k, h].astype(F32)

    def finish(k):
        for s in range(2):
            xcopy(2, s, k).wait_recv()
            xcopy(1, 1 - s, k).wait_recv()
            if k == 1:
                zhalf_copy(s).wait_recv()
            for h in range(2):
                value = line_sum(s, k, h)
                if k == 0 and s == 0:
                    zhalf[h] = value.astype(BF16)
                    start(zhalf_copy(h))
                elif k == 0:
                    own[h] = value
                else:
                    if k == 1 and h == s:
                        value = value + zhalf_in[s].astype(F32)
                    zsend[4 * s + k, h] = value.astype(BF16)
            if k > 0:
                start(zcopy(s, k))

    send_forward(0)
    send_forward(1)
    send_direct(0)
    send_forward(2)
    early.over_last()
    send_combined(0)
    send_direct(1)
    send_forward(3)
    send_combined(1)
    early.back()
    send_direct(2)
    finish(0)
    send_combined(2)
    send_direct(3)
    finish(1)
    send_combined(3)
    finish(2)
    finish(3)
    product = own[...]
    for k in range(1, 4):
        for s in range(2):
            zcopy(s, k).wait_recv()
            product = product + zrecv[s, k].astype(F32)
    product = product.reshape(2 * T, T)

    opened = product - prev_part[...]
    image.part[...] = dot(vt[...], product, ((1,), (0,)))
    image.scatter()
    square.part[...] = dot(opened, opened, ((0,), (0,)))
    square.scatter()
    open_ref[...] = opened
    sent(gathered.at[pl.ds(0, 14)], ring_s.at[0])
    sent(others, pair_s.at[0])
    for kind, ref in enumerate((fwd, direct, comb)):
        sent(ref, x_s.at[kind])
    sent(zsend.at[pl.ds(0, 6)], z_s.at[0])
    sent(zhalf, zh_s.at[0])
    early.collect()
    early.drain(range(4))
    early_ref[...] = early.totals[...]
    square.over_y()
    image.over_y()
    square.over_last()
    image.over_last()
    image.back()
    square.back()
    image.drain(range(3))
    square.drain(range(3))
    image.collect()
    square.collect()
    late_ref[0:T] = image.totals[...]
    late_ref[T : 2 * T] = square.totals[...]

    image.drain((3,))
    square.drain((3,))


def sum_scratch(rows, group, last):
    size = rows // group
    counts = (group, NY, last)
    return (
        [pltpu.VMEM((rows, T), F32)] * 2
        + [pltpu.VMEM((n, size, T), F32) for n in counts]
        + [pltpu.VMEM((size, T), F32)] * 3
        + [pltpu.SemaphoreType.DMA((4,))] * 2
    )


def communicate(rows, cols, count, v, vp, coupling, tiles):
    vmem = pl.BlockSpec(memory_space=pltpu.VMEM)
    dma = pltpu.SemaphoreType.DMA
    pair = (2, 4, 2, T, T)
    return pl.pallas_call(
        step_kernel,
        out_shape=(
            jax.ShapeDtypeStruct((2 * T, T), F32),
            jax.ShapeDtypeStruct((2 * T, T), F32),
            jax.ShapeDtypeStruct((2 * T, T), F32),
        ),
        in_specs=[pl.BlockSpec(memory_space=pl.ANY)] * 7,
        out_specs=(vmem, vmem, vmem),
        scratch_shapes=[
            pltpu.SMEM((SLOTS,), jnp.int32),
            pltpu.SMEM((SLOTS,), jnp.int32),
            pltpu.SMEM((1,), jnp.int32),
            pltpu.VMEM((2 * T, T), F32),
            pltpu.VMEM((2 * T, T), F32),
            pltpu.VMEM((T, T), F32),
            pltpu.VMEM((SLOTS, T, T), BF16),
            dma((7,)),
            pltpu.SMEM((NX * NZ * 2,), jnp.int32),
            pltpu.SMEM((SLOTS,), jnp.int32),
            pltpu.VMEM((2, T, T), BF16),
            pltpu.VMEM((2 * SLOTS, T, T), BF16),
            pltpu.VMEM((SLOTS + 1, T, T), F32),
            pltpu.VMEM((SLOTS + 1, T, T), BF16),
            pltpu.VMEM((2 * T, T), F32),
            pltpu.VMEM((T, 2 * T), F32),
        ]
        + [pltpu.VMEM(pair, BF16)] * 6
        + [
            pltpu.VMEM((2, T, T), F32),
            pltpu.VMEM((8, 2, T, T), BF16),
            pltpu.VMEM(pair, BF16),
            pltpu.VMEM((2, T, T), BF16),
            pltpu.VMEM((2, T, T), BF16),
            dma((1,)), dma((2, 4, 2)), dma((1,)), dma((1,)),
            dma((3,)), dma((3, 2, 4)), dma((1,)), dma((2, 4)), dma((1,)), dma((2,)),
        ]
        + sum_scratch(T, NZ * NC, NX)
        + sum_scratch(T, NX * NC, NZ)
        + sum_scratch(2 * T, NZ * NC, NX),
        compiler_params=pltpu.CompilerParams(collective_id=0, has_side_effects=True),
        name="krylov_step",
    )(rows, cols, count, v, vp, coupling, tiles)


def factor_kernel(total, late_ref, early_ref, open_ref, v_ref, basis_ref, projection_ref, rfactor_ref, residual, inverse_ref):
    image = late_ref[0:T]
    along = image * (1.0 / total)
    projection_ref[...] = image * total ** (-0.5)
    residual[...] = open_ref[...] - dot(v_ref[...], along, ((1,), (0,)))
    inner = (image - early_ref[T : 2 * T]) * (1.0 / total)
    inner = inner - 0.5 * dot(early_ref[0:T] * (1.0 / total), along, ((1,), (0,)))
    cross = dot(along, inner, ((0,), (0,)))
    gram = late_ref[T : 2 * T] * (1.0 / total) - cross - cross.T
    lane = lax.broadcasted_iota(jnp.int32, (1, T), 1)
    groups = T // 8
    left = [gram[8 * i : 8 * i + 8] for i in range(groups)]
    sub8 = lax.broadcasted_iota(jnp.int32, (8, T), 0)
    lane8 = lax.broadcasted_iota(jnp.int32, (8, T), 1)
    right = [jnp.where(lane8 == sub8 + 8 * i, 1.0, 0.0).astype(F32) for i in range(groups)]

    def spread(row):
        return jnp.broadcast_to(row, (8, T))

    def mix(rows, weight):
        value = None
        for j in range(8):
            term = weight[j] * rows[j]
            value = term if value is None else value + term
        return value

    for p in range(groups):
        panel, other = left[p], right[p]
        columns = [jnp.broadcast_to(panel[:, 8 * p + j : 8 * p + j + 1], (8, T)) for j in range(8)]
        a = [[spread(columns[j][i : i + 1]) for j in range(i + 1)] for i in range(8)]
        low = [[None] * 8 for _ in range(8)]
        inv = [None] * 8
        rows_l = [spread(panel[j : j + 1]) for j in range(8)]
        rows_r = [spread(other[j : j + 1]) for j in range(8)]
        for j in range(8):
            inv[j] = lax.rsqrt(a[j][j])
            for i in range(j + 1, 8):
                low[i][j] = a[i][j] * inv[j]
            for i in range(j + 1, 8):
                for k in range(j + 1, i + 1):
                    a[i][k] = a[i][k] - low[i][j] * low[k][j]
            rows_l[j] = rows_l[j] * inv[j]
            rows_r[j] = rows_r[j] * inv[j]
            for i in range(j + 1, 8):
                rows_l[i] = rows_l[i] - low[i][j] * rows_l[j]
                rows_r[i] = rows_r[i] - low[i][j] * rows_r[j]
        for i in range(8):
            r = 8 * p + i
            rfactor_ref[pl.ds(r, 1)] = jnp.where(lane >= r, rows_l[i][0:1], 0.0)
            inverse_ref[pl.ds(r, 1)] = rows_r[i][0:1]
        if p + 1 < groups:
            back_l, back_r = [None] * 8, [None] * 8
            for j in range(7, -1, -1):
                sum_l, sum_r = rows_l[j], rows_r[j]
                for i in range(j + 1, 8):
                    sum_l = sum_l - low[i][j] * back_l[i]
                    sum_r = sum_r - low[i][j] * back_r[i]
                back_l[j] = sum_l * inv[j]
                back_r[j] = sum_r * inv[j]
            for g in range(p + 1, groups):
                cols = [jnp.broadcast_to(left[g][:, 8 * p + j : 8 * p + j + 1], (8, T)) for j in range(8)]
                left[g] = left[g] - mix(back_l, cols)
                right[g] = right[g] - mix(back_r, cols)
    basis_ref[...] = dot(residual[...], inverse_ref[...], ((1,), (1,)))


def factor(total, late, early, opened, v):
    vmem = pl.BlockSpec(memory_space=pltpu.VMEM)
    return pl.pallas_call(
        functools.partial(factor_kernel, total),
        out_shape=(
            jax.ShapeDtypeStruct((2 * T, T), F32),
            jax.ShapeDtypeStruct((T, T), F32),
            jax.ShapeDtypeStruct((T, T), F32),
        ),
        in_specs=[vmem] * 4,
        out_specs=(vmem,) * 3,
        scratch_shapes=[pltpu.VMEM((2 * T, T), F32), pltpu.VMEM((T, T), F32)],
        name="factor",
    )(late, early, opened, v)


def on_device(basis_now, basis_prev, coupling, tiles, tile_rows, tile_cols, tile_counts):
    opened, late, early = communicate(
        tile_rows[0, 0], tile_cols[0, 0], tile_counts[0], basis_now, basis_prev, coupling, tiles[0, 0]
    )
    total = float(NX * NZ * NY * NC * 2 * T)
    return factor(total, late, early, opened, basis_now)


def solution(mesh):
    placed = (
        P(("row", "col"), None),
        P(("row", "col"), None),
        P(),
        P("row", "col", None, None, None),
        P("row", "col", None),
        P("row", "col", None),
        P("row", "col"),
    )
    return jax.shard_map(
        on_device,
        mesh=mesh,
        in_specs=placed,
        out_specs=(P(("row", "col"), None), P(), P()),
        check_vma=False,
    )
```
